256 devices in a mesh: space: 8 (over y, core), tm: 32 (over x, z).
Axes of the slice: x: 4, y: 4, z: 8, core: 2. Of those that a mesh axis runs over, the one named last changes fastest.
Arguments:
- snapshots: bfloat16 [8192, 32768], P('space', 'tm'), may hold values from -6 to 6
- basis: bfloat16 [8192, 64], P('space'), may hold values from -0.0625 to 0.0625
- lengths: int32 [16], replicated, may hold values from 1540 to 2048
Outputs:
- gram_matrix: float32 [2144, 2144], P('space')
- right_sides: float32 [2144, 64], P('space')
The draws below stay inside these ranges and needn't reach their ends.
Inputs may be any that keep to these rules, and one draw needn't show every extreme that they name: lengths[k] snapshots of trajectory k are recorded; later positions of its slot of 2048 are padding.
All inputs are finite; a program needn't handle non-finite values.
Results may differ from the reference program's by a relative error of at most 0.0003.
Values sent between devices are 32-bit elements; how exact they have to be, the bound alone decides.
No kernel may reach another device: no remote copies, remote signals or barrier semaphores. Data moves between devices by JAX's collectives and lax.ppermute only.
A program may use at most 64 MiB of HBM per device.

```python
import jax
import jax.numpy as jnp
import numpy as np
from jax import lax

R = 64
CELLS = 8192
T_DEV = 1024
TIMES = 32768
SLOT = 2048
TRAJ = 16


def with_ends(values, own_key, least, high):
    spot = [jax.random.randint(jax.random.fold_in(own_key, axis), (), 0, length) for axis, length in enumerate(values.shape)]
    longest = values.shape.index(max(values.shape))
    beside = spot[:longest] + [(spot[longest] + 1) % values.shape[longest]] + spot[longest + 1:]
    return values.at[tuple(spot)].set(least).at[tuple(beside)].set(high)


def steps_of(stream_key, shape, shards, least, top_value):
    level, own = 1.0, jax.random.fold_in(stream_key, 6)
    for dim, parts in shards:
        heights = jnp.exp(jax.random.uniform(jax.random.fold_in(own, dim), (parts,), jnp.float32, least / len(shards), top_value / len(shards)))
        level = level * jnp.repeat(heights, shape[dim] // parts).reshape([-1 if axis == dim else 1 for axis in range(len(shape))])
    return level


def normal_values(own_key, dims, scale, reach, shards=(), kind=jnp.bfloat16):
    values = scale * jax.random.normal(own_key, dims, jnp.float32)
    if shards:
        values = values * steps_of(own_key, dims, shards, -0.22, 0.18)
    return jnp.clip(values, -reach, reach).astype(kind)


def setup_inputs(seed: int = 0) -> dict:
    key_list = jax.random.split(jax.random.key(seed), 4)
    return {
        "snapshots": normal_values(key_list[0], (CELLS, TIMES), 1.0, 6.0, ((0, 8), (1, 32))),
        "basis": normal_values(key_list[1], (CELLS, R), CELLS ** -0.5, 0.0625, ((0, 8),)),
        "lengths": with_ends(jax.random.randint(key_list[2], (TRAJ,), T_DEV + T_DEV // 2 + 4, 2 * T_DEV + 1), jax.random.fold_in(key_list[2], 1), T_DEV + T_DEV // 2 + 4, 2 * T_DEV).astype(jnp.int32),
    }


EXACT = lax.Precision.HIGHEST

def features(block_rows):
    firsts, seconds = np.triu_indices(R)
    return jnp.concatenate([block_rows, block_rows[:, firsts] * block_rows[:, seconds]], axis=1)

def reference(snapshots, basis, lengths):
    states = jnp.dot(basis.T, snapshots, preferred_element_type=jnp.float32)
    horizon = states.shape[1]
    padded = jnp.pad(states, ((0, 0), (2, 2)))
    change = (padded[:, :horizon] - 8.0 * padded[:, 1:horizon + 1] + 8.0 * padded[:, 3:horizon + 3] - padded[:, 4:]) / 12.0
    shifted = jnp.arange(horizon, dtype=jnp.int32) + T_DEV // 2
    owners = (shifted // SLOT % lengths.shape[0]).astype(jnp.int32)
    offset = shifted % SLOT
    limits = lengths[owners]
    living = ((offset >= 2) & (offset <= limits - 3)).astype(jnp.float32)
    samples = jnp.sum(lengths - 4).astype(jnp.float32)
    masked = states * living[None, :]
    dmasked = change * living[None, :]
    energy = lax.optimization_barrier(jnp.sum(masked * masked, axis=1))
    scales = jnp.sqrt(energy / samples + 1e-06)
    scaled = (masked / scales[:, None]).T
    dscaled = (dmasked / scales[:, None]).T

    def step(totals, blocks):
        block_rows, block_change = blocks
        design = features(block_rows)
        gram_sum = totals[0] + jnp.dot(design.T, design, precision=EXACT, preferred_element_type=jnp.float32)
        side_sum = totals[1] + jnp.dot(design.T, block_change, precision=EXACT, preferred_element_type=jnp.float32)
        return ((gram_sum, side_sum), None)
    width_all = R * (R + 3) // 2
    initial = (jnp.zeros((width_all, width_all), jnp.float32), jnp.zeros((width_all, R), jnp.float32))
    pieces = horizon // T_DEV
    (gram_sum, side_sum), _ = lax.scan(step, initial, (scaled.reshape(pieces, T_DEV, R), dscaled.reshape(pieces, T_DEV, R)))
    return (gram_sum / samples, side_sum / samples)
```

```python
import functools

import jax
import jax.numpy as jnp
from jax import lax
from jax.experimental import pallas as pl
from jax.experimental.pallas import tpu as pltpu
from jax.sharding import Mesh, PartitionSpec as P

R = 64
FEAT = 2144
SLOT = 2048
TRAJ = 16
BLOCK = 1024
HALF = 512
ROWS = 268
ROWS_PAD = 272
COLS = 512
TAIL_QUADS = 96
TAIL_SIDES = 32
TAIL_ROWS = 144
PICKS = ROWS_PAD + COLS + TAIL_QUADS
TAIL_AT = 4 * ROWS_PAD
ENERGY_AT = TAIL_AT + TAIL_ROWS
PIECE = 160
TILES = 8 * PIECE
UP = 2.0**16


def swap(value):
    return lax.ppermute(value, "c", [(0, 1), (1, 0)])


def everyone(value, axis):
    count = lax.axis_size(axis)
    spread = jnp.broadcast_to(value[None], (count,) + value.shape)
    return lax.all_to_all(spread, axis, 0, 0, tiled=True)


def one_hots(first_feature, count):
    lane = lax.broadcasted_iota(jnp.int32, (count, 256), 1)
    feature = lax.broadcasted_iota(jnp.int32, (count, 256), 0) + first_feature
    mode = lane & (R - 1)
    below = lane < 3 * R
    ends = R + (mode + 1) * R - (mode + 1) * mode // 2
    passed = jnp.where((lane < R) & (feature >= ends), 1.0, 0.0)
    row = jnp.sum(passed, axis=1, keepdims=True).astype(jnp.int32)
    start = R + row * R - row * (row - 1) // 2
    linear = feature < R
    first = jnp.where(linear, feature, row)
    second = jnp.where(linear, -1, feature - start + row)
    pick_first = below & (mode == first)
    pick_second = (below & (mode == second)) | (linear & (lane == 3 * R))
    as_type = lambda pick: jnp.where(pick, 1.0, 0.0).astype(jnp.bfloat16)
    return as_type(pick_first), as_type(pick_second)


def split3(value):
    high = value.astype(jnp.bfloat16)
    rest = value - high.astype(jnp.float32)
    middle = rest.astype(jnp.bfloat16)
    low = (rest - middle.astype(jnp.float32)).astype(jnp.bfloat16)
    return high, middle, low


def split2(value):
    high = value.astype(jnp.bfloat16)
    return high, (value - high.astype(jnp.float32)).astype(jnp.bfloat16)


def dot(left, right, dims):
    return lax.dot_general(left, right, (dims, ((), ())), preferred_element_type=jnp.float32)


NT = ((1,), (1,))
NN = ((1,), (0,))


def gram_kernel(place, lengths, near, far, out, first_pick, second_pick, stack, change, rows_hi, rows_lo, cols_hi, cols_lo, acc, tail, energy):
    step = pl.program_id(0)
    last = pl.num_programs(0) - 1
    space, x, z = place[0], place[1], place[2]

    @pl.when(step == 0)
    def _():
        for at, count, feature in (
            (0, ROWS_PAD, space * ROWS),
            (ROWS_PAD, COLS, x * COLS),
            (ROWS_PAD + COLS, TAIL_QUADS, 4 * COLS),
        ):
            first, second = one_hots(feature, count)
            first_pick[at : at + count, :] = first
            second_pick[at : at + count, :] = second
        index = lax.broadcasted_iota(jnp.int32, (R, BLOCK), 0)
        stack[3 * R :, :] = jnp.where(index == 0, 1.0, 0.0).astype(jnp.bfloat16)
        acc[...] = jnp.zeros_like(acc)
        tail[...] = jnp.zeros_like(tail)
        energy[...] = jnp.zeros_like(energy)

    start = (step * 8 + z) * BLOCK
    states = jnp.concatenate([near[0, 0, :R, :], far[0, 0, :R, :]], axis=1) * UP
    ends = (near[0, 0, R:, :128] + far[0, 0, R:, :128]).T[:R, :] * UP
    lane = lax.broadcasted_iota(jnp.int32, (1, BLOCK), 1)
    position = (start + HALF) % SLOT
    one = lengths[(start + HALF) // SLOT % TRAJ]
    two = lengths[(start + 2 * HALF) // SLOT % TRAJ]
    offset = (position + lane) & (SLOT - 1)
    limit = jnp.where(lane < HALF, one, two) - 3
    living = jnp.where((offset >= 2) & (offset <= limit), 1.0, 0.0)
    wide = lax.broadcasted_iota(jnp.int32, (R, BLOCK), 1)
    before = jnp.where(wide == 0, ends[:, 1:2], pltpu.roll(states, 1, 1))
    before2 = jnp.where(wide == 0, ends[:, 0:1], jnp.where(wide == 1, ends[:, 1:2], pltpu.roll(states, 2, 1)))
    after = jnp.where(wide == BLOCK - 1, ends[:, 2:3], pltpu.roll(states, BLOCK - 1, 1))
    after2 = jnp.where(
        wide == BLOCK - 1, ends[:, 3:4], jnp.where(wide == BLOCK - 2, ends[:, 2:3], pltpu.roll(states, BLOCK - 2, 1))
    )
    change[...] = (before2 - 8.0 * before + 8.0 * after - after2) * (1.0 / 12.0) * living
    masked = states * living
    squares = masked * masked
    energy[...] += functools.reduce(lambda a, b: a + b, [squares[:, k * 128 : (k + 1) * 128] for k in range(BLOCK // 128)])
    high, middle, low = split3(masked)
    stack[:R, :] = high
    stack[R : 2 * R, :] = middle
    stack[2 * R : 3 * R, :] = low

    def features(at, count):
        first = dot(first_pick[at : at + count, :], stack[...], NN)
        second = dot(second_pick[at : at + count, :], stack[...], NN)
        return split2(first * second)

    rows_hi[...], rows_lo[...] = features(0, ROWS_PAD)
    for at in range(0, COLS, 256):
        cols_hi[at : at + 256, :], cols_lo[at : at + 256, :] = features(ROWS_PAD + at, 256)
    cols_hi[COLS : COLS + TAIL_QUADS, :], cols_lo[COLS : COLS + TAIL_QUADS, :] = features(ROWS_PAD + COLS, TAIL_QUADS)
    side = change[pl.ds(pl.multiple_of(x // 2 * TAIL_SIDES, TAIL_SIDES), TAIL_SIDES), :]
    cols_hi[COLS + TAIL_QUADS :, :], cols_lo[COLS + TAIL_QUADS :, :] = split2(side)

    for at in range(0, COLS, 256):
        left_hi, left_lo = rows_hi[...], rows_lo[...]
        right_hi, right_lo = cols_hi[at : at + 256, :], cols_lo[at : at + 256, :]
        acc[:, at : at + 256] += dot(left_hi, right_hi, NT) + (dot(left_hi, right_lo, NT) + dot(left_lo, right_hi, NT))
    part = pl.ds(pl.multiple_of(x % 2 * 128, 128), TAIL_ROWS)
    left_hi, left_lo = rows_hi[part, :], rows_lo[part, :]
    right_hi, right_lo = cols_hi[COLS:, :], cols_lo[COLS:, :]
    tail[...] += dot(left_hi, right_hi, NT) + (dot(left_hi, right_lo, NT) + dot(left_lo, right_hi, NT))

    @pl.when(step == last)
    def _():
        for k in range(COLS // 128):
            out[k * ROWS_PAD : (k + 1) * ROWS_PAD, :] = acc[:, k * 128 : (k + 1) * 128]
        out[TAIL_AT:ENERGY_AT, :] = tail[...]
        out[ENERGY_AT:, :] = jnp.zeros((TILES - ENERGY_AT, 128), jnp.float32)
        total = lax.dot_general(
            jnp.ones((8, 128), jnp.float32),
            energy[...],
            (NT, ((), ())),
            precision=lax.Precision.HIGHEST,
            preferred_element_type=jnp.float32,
        )
        out[ENERGY_AT : ENERGY_AT + 8, :R] = total


def gram(place, lengths, near, far):
    return pl.pallas_call(
        gram_kernel,
        out_shape=jax.ShapeDtypeStruct((TILES, 128), jnp.float32),
        grid_spec=pltpu.PrefetchScalarGridSpec(
            num_scalar_prefetch=2,
            grid=(4,),
            in_specs=[
                pl.BlockSpec((1, 1, R + 8, HALF), lambda i, *_: (0, i, 0, 0)),
                pl.BlockSpec((1, 1, R + 8, HALF), lambda i, *_: (0, i, 0, 0)),
            ],
            out_specs=pl.BlockSpec((TILES, 128), lambda i, *_: (0, 0)),
            scratch_shapes=[
                pltpu.VMEM((PICKS, 256), jnp.bfloat16),
                pltpu.VMEM((PICKS, 256), jnp.bfloat16),
                pltpu.VMEM((4 * R, BLOCK), jnp.bfloat16),
                pltpu.VMEM((R, BLOCK), jnp.float32),
                pltpu.VMEM((ROWS_PAD, BLOCK), jnp.bfloat16),
                pltpu.VMEM((ROWS_PAD, BLOCK), jnp.bfloat16),
                pltpu.VMEM((COLS + 128, BLOCK), jnp.bfloat16),
                pltpu.VMEM((COLS + 128, BLOCK), jnp.bfloat16),
                pltpu.VMEM((ROWS_PAD, COLS), jnp.float32),
                pltpu.VMEM((TAIL_ROWS, 128), jnp.float32),
                pltpu.VMEM((R, 128), jnp.float32),
            ],
        ),
        name="gram",
    )(place, lengths, near, far)


def scale_kernel(place, lengths, block, out):
    space, x = place[0], place[1]
    samples = lengths[0] - 4
    for k in range(1, TRAJ):
        samples += lengths[k] - 4
    samples = samples.astype(jnp.float32)
    energy = block[ENERGY_AT : ENERGY_AT + 8, :R] * (1.0 / (UP * UP))
    inverse = (1.0 / UP) / jnp.sqrt(energy / samples + 1e-06)
    high, middle, low = split3(inverse)
    fill = jnp.where(lax.broadcasted_iota(jnp.int32, (8, R), 1) == 0, 1.0, 0.0).astype(jnp.bfloat16)
    weights = jnp.concatenate([high.astype(jnp.float32), middle.astype(jnp.float32), low.astype(jnp.float32), fill.astype(jnp.float32)], axis=1)
    weights = weights.astype(jnp.bfloat16)
    tall = jnp.broadcast_to(weights[0:1, :].astype(jnp.float32), (128, 256)).astype(jnp.bfloat16)
    first, second = one_hots(space * ROWS, ROWS_PAD)
    row_weight = dot(first, tall, NT) * dot(second, tall, NT)
    by_row = row_weight / samples
    for k in range(COLS // 128):
        first, second = one_hots(x * COLS + k * 128, 128)
        column = (dot(weights, first, NT) * dot(weights, second, NT))[0:1, :]
        out[k * ROWS_PAD : (k + 1) * ROWS_PAD, :] = block[k * ROWS_PAD : (k + 1) * ROWS_PAD, :] * by_row * column
    first, second = one_hots(4 * COLS, TAIL_QUADS)
    quads = (dot(weights, first, NT) * dot(weights, second, NT))[0:1, :]
    low_sides, high_sides = inverse[0:1, :TAIL_SIDES], inverse[0:1, TAIL_SIDES:]
    sides = jnp.where(x < 2, low_sides, high_sides)
    column = jnp.concatenate([quads, sides], axis=1)
    tail_rows = jnp.where(x % 2 == 0, by_row[:TAIL_ROWS, :], by_row[128:, :])
    out[TAIL_AT:ENERGY_AT, :] = block[TAIL_AT:ENERGY_AT, :] * tail_rows * column
    out[ENERGY_AT:, :] = jnp.zeros((TILES - ENERGY_AT, 128), jnp.float32)


def scale(place, lengths, block):
    return pl.pallas_call(
        scale_kernel,
        out_shape=jax.ShapeDtypeStruct((TILES, 128), jnp.float32),
        grid_spec=pltpu.PrefetchScalarGridSpec(
            num_scalar_prefetch=2,
            grid=(1,),
            in_specs=[pl.BlockSpec((TILES, 128), lambda i, *_: (0, 0))],
            out_specs=pl.BlockSpec((TILES, 128), lambda i, *_: (0, 0)),
        ),
        name="scale",
    )(place, lengths, block)


def lay_kernel(parts, gram_out, side_out):
    for x in range(4):
        for k in range(4):
            lanes = (4 * x + k) * 128
            gram_out[:, lanes : lanes + 128] = parts[x, k * ROWS_PAD : k * ROWS_PAD + ROWS, :]
    split = 128
    for x, at, to in ((0, 0, 0), (1, 0, split)):
        count = split if x == 0 else ROWS - split
        gram_out[to : to + count, 16 * 128 :] = parts[x, TAIL_AT : TAIL_AT + count, :TAIL_QUADS]
        side_out[to : to + count, :TAIL_SIDES] = parts[x, TAIL_AT : TAIL_AT + count, TAIL_QUADS:]
        side_out[to : to + count, TAIL_SIDES:] = parts[x + 2, TAIL_AT : TAIL_AT + count, TAIL_QUADS:]


def lay(parts):
    return pl.pallas_call(
        lay_kernel,
        out_shape=(
            jax.ShapeDtypeStruct((ROWS, FEAT), jnp.float32),
            jax.ShapeDtypeStruct((ROWS, R), jnp.float32),
        ),
        name="lay",
    )(parts)


def shards(snapshots, basis, lengths):
    core, x, z = lax.axis_index("c"), lax.axis_index("x"), lax.axis_index("z")
    space = lax.axis_index("y") * 2 + core
    place = jnp.stack([space, x, z, core]).astype(jnp.int32)
    partial = jnp.einsum("cr,ct->rt", basis, snapshots, preferred_element_type=jnp.float32)
    head = partial[:, :2].T
    tail = partial[:, BLOCK - 2 :].T
    left = lax.ppermute(tail, ("x", "z"), [(i, i + 1) for i in range(31)])
    right = lax.ppermute(head, ("x", "z"), [(i + 1, i) for i in range(31)])
    mine = lax.dynamic_slice_in_dim(partial, core * HALF, HALF, 1)
    other = lax.dynamic_slice_in_dim(partial, (1 - core) * HALF, HALF, 1)
    half = mine + swap(other)
    ends = jnp.pad(jnp.concatenate([left, right], axis=0), ((0, 4), (0, HALF - R)))
    message = jnp.sum(everyone(jnp.concatenate([half, ends], axis=0), "y").reshape(4, R + 8, HALF), axis=0)
    own = everyone(message, "x").reshape(4, R + 8, HALF)
    theirs = swap(own)
    near = jnp.where(core == 0, own, theirs)[None]
    far = jnp.where(core == 0, theirs, own)[None]
    block = gram(place, lengths, near, far)
    piece = jnp.sum(lax.all_to_all(block.reshape(8, PIECE, 128), "z", 0, 0, tiled=True), axis=0)
    block = everyone(piece, "z").reshape(TILES, 128)
    block = scale(place, lengths, block)
    parts = everyone(block, "x").reshape(4, TILES, 128)
    return lay(parts)


def solution(mesh):
    grid = Mesh(mesh.devices.reshape(4, 2, 4, 8), ("y", "c", "x", "z"))
    return jax.shard_map(
        shards,
        mesh=grid,
        in_specs=(P(("y", "c"), ("x", "z")), P(("y", "c"), None), P()),
        out_specs=(P(("y", "c"), None), P(("y", "c"), None)),
        check_vma=False,
    )
```

```python
import functools

import jax
import jax.numpy as jnp
from jax import lax
from jax.experimental import pallas as pl
from jax.experimental.pallas import tpu as pltpu
from jax.sharding import Mesh, PartitionSpec as P

R = 64
FEAT = 2144
SLOT = 2048
TRAJ = 16
BLOCK = 1024
HALF = 512
ROWS = 268
ROWS_PAD = 272
COLS = 512
TAIL_QUADS = 96
TAIL_SIDES = 32
TAIL_ROWS = 144
PICKS = ROWS_PAD + COLS + TAIL_QUADS
TAIL_AT = 4 * ROWS_PAD
ENERGY_AT = TAIL_AT + TAIL_ROWS
PIECE = 160
TILES = 8 * PIECE
UP = 2.0**16


def swap(value):
    return lax.ppermute(value, "c", [(0, 1), (1, 0)])


def turn(value, axis, by):
    count = lax.axis_size(axis)
    return lax.ppermute(value, axis, [(i, (i + by) % count) for i in range(count)])


def near_by(value):
    return pltpu.with_memory_space_constraint(value, pltpu.VMEM)


def everyone(value, axis):
    count = lax.axis_size(axis)
    spread = jnp.broadcast_to(value[None], (count,) + value.shape)
    return lax.all_to_all(spread, axis, 0, 0, tiled=True)


def one_hots(first_feature, count):
    lane = lax.broadcasted_iota(jnp.int32, (count, 256), 1)
    feature = lax.broadcasted_iota(jnp.int32, (count, 256), 0) + first_feature
    mode = lane & (R - 1)
    below = lane < 3 * R
    ends = R + (mode + 1) * R - (mode + 1) * mode // 2
    passed = jnp.where((lane < R) & (feature >= ends), 1.0, 0.0)
    row = jnp.sum(passed, axis=1, keepdims=True).astype(jnp.int32)
    start = R + row * R - row * (row - 1) // 2
    linear = feature < R
    first = jnp.where(linear, feature, row)
    second = jnp.where(linear, -1, feature - start + row)
    pick_first = below & (mode == first)
    pick_second = (below & (mode == second)) | (linear & (lane == 3 * R))
    as_type = lambda pick: jnp.where(pick, 1.0, 0.0).astype(jnp.bfloat16)
    return as_type(pick_first), as_type(pick_second)


def split3(value):
    high = value.astype(jnp.bfloat16)
    rest = value - high.astype(jnp.float32)
    middle = rest.astype(jnp.bfloat16)
    low = (rest - middle.astype(jnp.float32)).astype(jnp.bfloat16)
    return high, middle, low


def split2(value):
    high = value.astype(jnp.bfloat16)
    return high, (value - high.astype(jnp.float32)).astype(jnp.bfloat16)


def dot(left, right, dims):
    return lax.dot_general(left, right, (dims, ((), ())), preferred_element_type=jnp.float32)


NT = ((1,), (1,))
NN = ((1,), (0,))


def pick_kernel(place, first_pick, second_pick):
    space, x = place[0], place[1]
    for at, count, feature in (
        (0, ROWS_PAD, space * ROWS),
        (ROWS_PAD, COLS, x * COLS),
        (ROWS_PAD + COLS, TAIL_QUADS, 4 * COLS),
    ):
        first, second = one_hots(feature, count)
        first_pick[at : at + count, :] = first
        second_pick[at : at + count, :] = second


SMEM = pl.BlockSpec(memory_space=pltpu.SMEM)
VMEM = pl.BlockSpec(memory_space=pltpu.VMEM)


def picks(place):
    return pl.pallas_call(
        pick_kernel,
        out_shape=(pltpu.VMEM((PICKS, 256), jnp.bfloat16), pltpu.VMEM((PICKS, 256), jnp.bfloat16)),
        in_specs=[SMEM],
        out_specs=(VMEM, VMEM),
        name="picks",
    )(place)


def gram_kernel(place, lengths, first_pick, second_pick, *rest):
    mine, theirs = rest[:4], rest[4:8]
    out, stack, change, rows_hi, rows_lo, cols_hi, cols_lo, acc, tail, energy = rest[8:]
    x, z, core = place[1], place[2], place[3]
    index = lax.broadcasted_iota(jnp.int32, (R, BLOCK), 0)
    stack[3 * R :, :] = jnp.where(index == 0, 1.0, 0.0).astype(jnp.bfloat16)
    lane = lax.broadcasted_iota(jnp.int32, (1, BLOCK), 1)
    wide = lax.broadcasted_iota(jnp.int32, (R, BLOCK), 1)

    def features(at, count):
        first = dot(first_pick[at : at + count, :], stack[...], NN)
        second = dot(second_pick[at : at + count, :], stack[...], NN)
        return split2(first * second)

    for step in range(4):
        start = ((x + step) % 4 * 8 + z) * BLOCK
        own, other = mine[step], theirs[step]
        near = jnp.where(core == 0, own[:R, :], other[:R, :])
        far = jnp.where(core == 0, other[:R, :], own[:R, :])
        states = jnp.concatenate([near, far], axis=1) * UP
        ends = (own[R:, :128] + other[R:, :128]).T[:R, :] * UP
        position = (start + HALF) % SLOT
        one = lengths[(start + HALF) // SLOT % TRAJ]
        two = lengths[(start + 2 * HALF) // SLOT % TRAJ]
        offset = (position + lane) & (SLOT - 1)
        limit = jnp.where(lane < HALF, one, two) - 3
        living = jnp.where((offset >= 2) & (offset <= limit), 1.0, 0.0)
        before = jnp.where(wide == 0, ends[:, 1:2], pltpu.roll(states, 1, 1))
        before2 = jnp.where(wide == 0, ends[:, 0:1], jnp.where(wide == 1, ends[:, 1:2], pltpu.roll(states, 2, 1)))
        after = jnp.where(wide == BLOCK - 1, ends[:, 2:3], pltpu.roll(states, BLOCK - 1, 1))
        after2 = jnp.where(
            wide == BLOCK - 1, ends[:, 3:4], jnp.where(wide == BLOCK - 2, ends[:, 2:3], pltpu.roll(states, BLOCK - 2, 1))
        )
        change[...] = (before2 - 8.0 * before + 8.0 * after - after2) * (1.0 / 12.0) * living
        masked = states * living
        squares = masked * masked
        square = functools.reduce(lambda a, b: a + b, [squares[:, k * 128 : (k + 1) * 128] for k in range(BLOCK // 128)])
        energy[...] = square if step == 0 else energy[...] + square
        stack[:R, :], stack[R : 2 * R, :], stack[2 * R : 3 * R, :] = split3(masked)

        rows_hi[...], rows_lo[...] = features(0, ROWS_PAD)
        for at in range(0, COLS, 256):
            cols_hi[at : at + 256, :], cols_lo[at : at + 256, :] = features(ROWS_PAD + at, 256)
        cols_hi[COLS : COLS + TAIL_QUADS, :], cols_lo[COLS : COLS + TAIL_QUADS, :] = features(ROWS_PAD + COLS, TAIL_QUADS)
        side = change[pl.ds(pl.multiple_of(x // 2 * TAIL_SIDES, TAIL_SIDES), TAIL_SIDES), :]
        cols_hi[COLS + TAIL_QUADS :, :], cols_lo[COLS + TAIL_QUADS :, :] = split2(side)

        for at in range(0, COLS, 256):
            left_hi, left_lo = rows_hi[...], rows_lo[...]
            right_hi, right_lo = cols_hi[at : at + 256, :], cols_lo[at : at + 256, :]
            total = dot(left_hi, right_hi, NT) + (dot(left_hi, right_lo, NT) + dot(left_lo, right_hi, NT))
            acc[:, at : at + 256] = total if step == 0 else acc[:, at : at + 256] + total
        part = pl.ds(pl.multiple_of(x % 2 * 128, 128), TAIL_ROWS)
        left_hi, left_lo = rows_hi[part, :], rows_lo[part, :]
        right_hi, right_lo = cols_hi[COLS:, :], cols_lo[COLS:, :]
        total = dot(left_hi, right_hi, NT) + (dot(left_hi, right_lo, NT) + dot(left_lo, right_hi, NT))
        tail[...] = total if step == 0 else tail[...] + total

    for k in range(COLS // 128):
        out[k * ROWS_PAD : (k + 1) * ROWS_PAD, :] = acc[:, k * 128 : (k + 1) * 128]
    out[TAIL_AT:ENERGY_AT, :] = tail[...]
    out[ENERGY_AT:, :] = jnp.zeros((TILES - ENERGY_AT, 128), jnp.float32)
    out[ENERGY_AT : ENERGY_AT + 8, :R] = lax.dot_general(
        jnp.ones((8, 128), jnp.float32),
        energy[...],
        (NT, ((), ())),
        precision=lax.Precision.HIGHEST,
        preferred_element_type=jnp.float32,
    )


def gram(place, lengths, first_pick, second_pick, mine, theirs):
    return pl.pallas_call(
        gram_kernel,
        out_shape=pltpu.VMEM((TILES, 128), jnp.float32),
        in_specs=[SMEM, SMEM] + [VMEM] * 10,
        out_specs=VMEM,
        scratch_shapes=[
            pltpu.VMEM((4 * R, BLOCK), jnp.bfloat16),
            pltpu.VMEM((R, BLOCK), jnp.float32),
            pltpu.VMEM((ROWS_PAD, BLOCK), jnp.bfloat16),
            pltpu.VMEM((ROWS_PAD, BLOCK), jnp.bfloat16),
            pltpu.VMEM((COLS + 128, BLOCK), jnp.bfloat16),
            pltpu.VMEM((COLS + 128, BLOCK), jnp.bfloat16),
            pltpu.VMEM((ROWS_PAD, COLS), jnp.float32),
            pltpu.VMEM((TAIL_ROWS, 128), jnp.float32),
            pltpu.VMEM((R, 128), jnp.float32),
        ],
        name="gram",
    )(place, lengths, *[near_by(v) for v in (first_pick, second_pick, *mine, *theirs)])


def scale_kernel(place, lengths, first_pick, second_pick, block, out):
    x = place[1]
    samples = lengths[0] - 4
    for k in range(1, TRAJ):
        samples += lengths[k] - 4
    samples = samples.astype(jnp.float32)
    energy = block[ENERGY_AT : ENERGY_AT + 8, :R] * (1.0 / (UP * UP))
    inverse = (1.0 / UP) / jnp.sqrt(energy / samples + 1e-06)
    high, middle, low = [part.astype(jnp.float32) for part in split3(inverse)]
    fill = jnp.where(lax.broadcasted_iota(jnp.int32, (8, R), 1) == 0, 1.0, 0.0)
    weights = jnp.concatenate([high, middle, low, fill], axis=1)
    tall = jnp.broadcast_to(weights[0:1, :], (128, 256)).astype(jnp.bfloat16)
    weights = weights.astype(jnp.bfloat16)
    by_row = dot(first_pick[:ROWS_PAD, :], tall, NT) * dot(second_pick[:ROWS_PAD, :], tall, NT) / samples
    by_column = (dot(weights, first_pick[ROWS_PAD:, :], NT) * dot(weights, second_pick[ROWS_PAD:, :], NT))[0:1, :]
    for k in range(COLS // 128):
        rows = slice(k * ROWS_PAD, (k + 1) * ROWS_PAD)
        out[rows, :] = block[rows, :] * by_row * by_column[:, k * 128 : (k + 1) * 128]
    sides = jnp.where(x < 2, inverse[0:1, :TAIL_SIDES], inverse[0:1, TAIL_SIDES:])
    column = jnp.concatenate([by_column[:, COLS:], sides], axis=1)
    tail_rows = jnp.where(x % 2 == 0, by_row[:TAIL_ROWS, :], by_row[128:, :])
    out[TAIL_AT:ENERGY_AT, :] = block[TAIL_AT:ENERGY_AT, :] * tail_rows * column
    out[ENERGY_AT:, :] = jnp.zeros((TILES - ENERGY_AT, 128), jnp.float32)


def scale(place, lengths, first_pick, second_pick, block):
    return pl.pallas_call(
        scale_kernel,
        out_shape=pltpu.VMEM((TILES, 128), jnp.float32),
        in_specs=[SMEM, SMEM, VMEM, VMEM, VMEM],
        out_specs=VMEM,
        name="scale",
    )(place, lengths, *[near_by(v) for v in (first_pick, second_pick, block)])


def lay_kernel(place, own, left, right, far_top, far_bottom, gram_out, side_out, tails):
    x = place[1]
    half = TILES // 2

    def put(source, at, parts):
        for k in range(4):
            first = k * ROWS_PAD
            lanes = pl.ds(pl.multiple_of((source * 4 + k) * 128, 128), 128)
            for part, low, high in parts:
                begin, end = max(first, low), min(first + ROWS, high)
                if begin < end:
                    gram_out[begin - first : end - first, lanes] = part[begin - low : end - low, :]
        for part, low, high in parts:
            begin, end = max(TAIL_AT, low), min(ENERGY_AT, high)
            if begin < end:
                tails[source, begin - TAIL_AT : end - TAIL_AT, :] = part[begin - low : end - low, :]

    put(x, 0, [(own, 0, TILES)])
    put((x + 3) % 4, 1, [(left, 0, TILES)])
    put((x + 1) % 4, 2, [(right, 0, TILES)])
    put((x + 2) % 4, 3, [(far_top, 0, half), (far_bottom, half, TILES)])
    for x_of, low, high in ((0, 0, 128), (1, 128, ROWS)):
        count = high - low
        gram_out[low:high, 16 * 128 :] = tails[x_of, :count, :TAIL_QUADS]
        sides = jnp.concatenate([tails[x_of, :count, TAIL_QUADS:], tails[x_of + 2, :count, TAIL_QUADS:]], axis=1)
        side_out[low:high, :] = sides


def lay(place, *pieces):
    return pl.pallas_call(
        lay_kernel,
        out_shape=(
            jax.ShapeDtypeStruct((ROWS, FEAT), jnp.float32),
            jax.ShapeDtypeStruct((ROWS, R), jnp.float32),
        ),
        in_specs=[SMEM] + [VMEM] * 5,
        out_specs=(VMEM, VMEM),
        scratch_shapes=[pltpu.VMEM((4, TAIL_ROWS, 128), jnp.float32)],
        name="lay",
    )(place, *[near_by(v) for v in pieces])


def shards(snapshots, basis, lengths):
    core, x, z = lax.axis_index("c"), lax.axis_index("x"), lax.axis_index("z")
    space = lax.axis_index("y") * 2 + core
    place = jnp.stack([space, x, z, core]).astype(jnp.int32)
    head = snapshots[:, :2].T.astype(jnp.float32)
    tail = snapshots[:, BLOCK - 2 :].T.astype(jnp.float32)
    left = lax.ppermute(tail, ("x", "z"), [(i, i + 1) for i in range(31)])
    right = lax.ppermute(head, ("x", "z"), [(i + 1, i) for i in range(31)])
    partial = jnp.einsum("cr,ct->rt", basis, snapshots, preferred_element_type=jnp.float32)
    mine = lax.dynamic_slice_in_dim(partial, core * HALF, HALF, 1)
    other = lax.dynamic_slice_in_dim(partial, (1 - core) * HALF, HALF, 1)
    half = mine + swap(other)
    ends = jnp.einsum(
        "tc,cr->tr",
        jnp.concatenate([left, right], axis=0),
        basis.astype(jnp.float32),
        precision=lax.Precision.HIGHEST,
        preferred_element_type=jnp.float32,
    )
    ends = jnp.pad(ends, ((0, 4), (0, HALF - R)))
    message = jnp.concatenate([half, ends], axis=0)
    message = (message + turn(message, "y", 2)) + (turn(message, "y", 1) + turn(message, "y", 3))
    mine = (message, turn(message, "x", 3), turn(message, "x", 2), turn(message, "x", 1))
    theirs = tuple(swap(part) for part in mine)
    first_pick, second_pick = picks(place)
    block = gram(place, lengths, first_pick, second_pick, mine, theirs)
    piece = jnp.sum(lax.all_to_all(block.reshape(8, PIECE, 128), "z", 0, 0, tiled=True), axis=0)
    block = everyone(piece, "z").reshape(TILES, 128)
    block = scale(place, lengths, first_pick, second_pick, block)
    half = TILES // 2
    from_left, from_right = turn(block, "x", 1), turn(block, "x", 3)
    far_top, far_bottom = turn(from_left[:half], "x", 1), turn(from_right[half:], "x", 3)
    return lay(place, block, from_left, from_right, far_top, far_bottom)


def solution(mesh):
    grid = Mesh(mesh.devices.reshape(4, 2, 4, 8), ("y", "c", "x", "z"))
    return jax.shard_map(
        shards,
        mesh=grid,
        in_specs=(P(("y", "c"), ("x", "z")), P(("y", "c"), None), P()),
        out_specs=(P(("y", "c"), None), P(("y", "c"), None)),
        check_vma=False,
    )
```

```python
import functools

import jax
import jax.numpy as jnp
from jax import lax
from jax.experimental import pallas as pl
from jax.experimental.pallas import tpu as pltpu
from jax.sharding import Mesh, PartitionSpec as P

R = 64
FEAT = 2144
SLOT = 2048
TRAJ = 16
BLOCK = 1024
HALF = 512
ROWS = 268
ROWS_PAD = 272
COLS = 512
TAIL_QUADS = 96
TAIL_SIDES = 32
TAIL_ROWS = 144
PICKS = ROWS_PAD + COLS + TAIL_QUADS
TAIL_AT = 4 * ROWS_PAD
ENERGY_AT = TAIL_AT + TAIL_ROWS
PIECE = 160
TILES = 8 * PIECE
UP = 2.0**16


def swap(value):
    return lax.ppermute(value, "c", [(0, 1), (1, 0)])


def turn(value, axis, by):
    count = lax.axis_size(axis)
    return lax.ppermute(value, axis, [(i, (i + by) % count) for i in range(count)])


def near_by(value):
    return pltpu.with_memory_space_constraint(value, pltpu.VMEM)


def everyone(value, axis):
    count = lax.axis_size(axis)
    spread = jnp.broadcast_to(value[None], (count,) + value.shape)
    return lax.all_to_all(spread, axis, 0, 0, tiled=True)


def one_hots(first_feature, count):
    lane = lax.broadcasted_iota(jnp.int32, (count, 256), 1)
    feature = lax.broadcasted_iota(jnp.int32, (count, 256), 0) + first_feature
    mode = lane & (R - 1)
    below = lane < 3 * R
    ends = R + (mode + 1) * R - (mode + 1) * mode // 2
    passed = jnp.where((lane < R) & (feature >= ends), 1.0, 0.0)
    row = jnp.sum(passed, axis=1, keepdims=True).astype(jnp.int32)
    start = R + row * R - row * (row - 1) // 2
    linear = feature < R
    first = jnp.where(linear, feature, row)
    second = jnp.where(linear, -1, feature - start + row)
    pick_first = below & (mode == first)
    pick_second = (below & (mode == second)) | (linear & (lane == 3 * R))
    as_type = lambda pick: jnp.where(pick, 1.0, 0.0).astype(jnp.bfloat16)
    return as_type(pick_first), as_type(pick_second)


def split3(value):
    high = value.astype(jnp.bfloat16)
    rest = value - high.astype(jnp.float32)
    middle = rest.astype(jnp.bfloat16)
    low = (rest - middle.astype(jnp.float32)).astype(jnp.bfloat16)
    return high, middle, low


def split2(value):
    high = value.astype(jnp.bfloat16)
    return high, (value - high.astype(jnp.float32)).astype(jnp.bfloat16)


def dot(left, right, dims):
    return lax.dot_general(left, right, (dims, ((), ())), preferred_element_type=jnp.float32)


NT = ((1,), (1,))
NN = ((1,), (0,))


def position():
    return lax.axis_index("c"), lax.axis_index("x"), lax.axis_index("z")


def pick_kernel(first_pick, second_pick):
    core, x, _ = position()
    space = lax.axis_index("y") * 2 + core
    for at, count, feature in (
        (0, ROWS_PAD, space * ROWS),
        (ROWS_PAD, COLS, x * COLS),
        (ROWS_PAD + COLS, TAIL_QUADS, 4 * COLS),
    ):
        first, second = one_hots(feature, count)
        first_pick[at : at + count, :] = first
        second_pick[at : at + count, :] = second


SMEM = pl.BlockSpec(memory_space=pltpu.SMEM)
VMEM = pl.BlockSpec(memory_space=pltpu.VMEM)
ROOM = pltpu.CompilerParams(vmem_limit_bytes=24 * 1024 * 1024)


def picks():
    return pl.pallas_call(
        pick_kernel,
        out_shape=(pltpu.VMEM((PICKS, 256), jnp.bfloat16), pltpu.VMEM((PICKS, 256), jnp.bfloat16)),
        out_specs=(VMEM, VMEM),
        compiler_params=ROOM,
        name="picks",
    )()


def whole_block(own, other, core):
    near = jnp.where(core == 0, own[...], other[...])
    far = jnp.where(core == 0, other[...], own[...])
    return jnp.concatenate([near, far], axis=1) * UP


def alive(lengths, start):
    lane = lax.broadcasted_iota(jnp.int32, (1, BLOCK), 1)
    one = lengths[(start + HALF) // SLOT % TRAJ]
    two = lengths[(start + 2 * HALF) // SLOT % TRAJ]
    offset = ((start + HALF) % SLOT + lane) & (SLOT - 1)
    limit = jnp.where(lane < HALF, one, two) - 3
    return jnp.where((offset >= 2) & (offset <= limit), 1.0, 0.0)


def features(first_pick, second_pick, stack, at, count):
    first = dot(first_pick[at : at + count, :], stack, NN)
    second = dot(second_pick[at : at + count, :], stack, NN)
    return split2(first * second)


def product(left_hi, left_lo, right_hi, right_lo):
    return dot(left_hi, right_hi, NT) + (dot(left_hi, right_lo, NT) + dot(left_lo, right_hi, NT))


def stacked(masked, stack):
    stack[:R, :], stack[R : 2 * R, :], stack[2 * R : 3 * R, :] = split3(masked)
    index = lax.broadcasted_iota(jnp.int32, masked.shape, 0)
    stack[3 * R :, :] = jnp.where(index == 0, 1.0, 0.0).astype(jnp.bfloat16)


def gram_kernel(lengths, first_pick, second_pick, *rest):
    mine, theirs = rest[:4], rest[4:8]
    out, stack, rows_hi, rows_lo, acc, energy = rest[8:]
    core, x, z = position()
    for step in range(4):
        start = ((x + step) % 4 * 8 + z) * BLOCK
        masked = whole_block(mine[step], theirs[step], core) * alive(lengths, start)
        squares = masked * masked
        square = functools.reduce(lambda a, b: a + b, [squares[:, k * 128 : (k + 1) * 128] for k in range(BLOCK // 128)])
        energy[...] = square if step == 0 else energy[...] + square
        stacked(masked, stack)
        rows_hi[...], rows_lo[...] = features(first_pick, second_pick, stack[...], 0, ROWS_PAD)
        for at in range(0, COLS, 256):
            right_hi, right_lo = features(first_pick, second_pick, stack[...], ROWS_PAD + at, 256)
            total = product(rows_hi[...], rows_lo[...], right_hi, right_lo)
            acc[:, at : at + 256] = total if step == 0 else acc[:, at : at + 256] + total
    for k in range(COLS // 128):
        out[k * ROWS_PAD : (k + 1) * ROWS_PAD, :] = acc[:, k * 128 : (k + 1) * 128]
    out[TAIL_AT:, :] = jnp.zeros((TILES - TAIL_AT, 128), jnp.float32)
    out[ENERGY_AT : ENERGY_AT + 8, :R] = lax.dot_general(
        jnp.ones((8, 128), jnp.float32),
        energy[...],
        (NT, ((), ())),
        precision=lax.Precision.HIGHEST,
        preferred_element_type=jnp.float32,
    )


def gram(lengths, first_pick, second_pick, mine, theirs):
    return pl.pallas_call(
        gram_kernel,
        out_shape=pltpu.VMEM((TILES, 128), jnp.float32),
        in_specs=[SMEM] + [VMEM] * 10,
        out_specs=VMEM,
        scratch_shapes=[
            pltpu.VMEM((4 * R, BLOCK), jnp.bfloat16),
            pltpu.VMEM((ROWS_PAD, BLOCK), jnp.bfloat16),
            pltpu.VMEM((ROWS_PAD, BLOCK), jnp.bfloat16),
            pltpu.VMEM((ROWS_PAD, COLS), jnp.float32),
            pltpu.VMEM((R, 128), jnp.float32),
        ],
        compiler_params=ROOM,
        name="gram",
    )(lengths, *[near_by(v) for v in (first_pick, second_pick, *mine, *theirs)])


def edge_kernel(*refs):
    parts, out = refs[:4], refs[4]
    core = lax.axis_index("c")
    lane = lax.broadcasted_iota(jnp.int32, (R, 128), 1)
    edges = jnp.zeros((R, 128), jnp.float32)
    for step, part in enumerate(parts):
        first, last = part[:, :128], pltpu.roll(part[:, HALF - 128 :], 2, 1)
        here = jnp.where(core == 0, first, last)
        edges = jnp.where((lane >> 1) == step, pltpu.roll(here, 2 * step, 1) if step else here, edges)
    out[...] = edges


def edges_of(parts):
    return pl.pallas_call(
        edge_kernel,
        out_shape=pltpu.VMEM((R, 128), jnp.float32),
        in_specs=[VMEM] * 4,
        out_specs=VMEM,
        compiler_params=ROOM,
        name="edges",
    )(*[near_by(v) for v in parts])


def tail_kernel(lengths, first_pick, second_pick, same, cross, *rest):
    mine, theirs = rest[:4], rest[4:8]
    block, out, stack, change, cols_hi, cols_lo, rows_hi, rows_lo, tail = rest[8:]
    core, x, z = position()
    wide = lax.broadcasted_iota(jnp.int32, (R, BLOCK), 1)
    lefts = jnp.where(core == 0, cross[...], same[...]) * UP
    rights = jnp.where(core == 0, same[...], cross[...]) * UP
    pair = lambda ends, step: ends[:, 2 * (step % 4) : 2 * (step % 4) + 2]
    part = pl.ds(pl.multiple_of(x % 2 * 128, 128), TAIL_ROWS)
    for step in range(4):
        where = (x + step) % 4
        start = (where * 8 + z) * BLOCK
        left = jnp.where(z == 0, pair(lefts, step + 3), pair(lefts, step))
        left = jnp.where((z == 0) & (where == 0), 0.0, left)
        right = jnp.where(z == 7, pair(rights, step + 1), pair(rights, step))
        right = jnp.where((z == 7) & (where == 3), 0.0, right)
        states = whole_block(mine[step], theirs[step], core)
        living = alive(lengths, start)
        before = jnp.where(wide == 0, left[:, 1:2], pltpu.roll(states, 1, 1))
        before2 = jnp.where(wide == 0, left[:, 0:1], jnp.where(wide == 1, left[:, 1:2], pltpu.roll(states, 2, 1)))
        after = jnp.where(wide == BLOCK - 1, right[:, 0:1], pltpu.roll(states, BLOCK - 1, 1))
        after2 = jnp.where(
            wide == BLOCK - 1, right[:, 1:2], jnp.where(wide == BLOCK - 2, right[:, 0:1], pltpu.roll(states, BLOCK - 2, 1))
        )
        change[...] = (before2 - 8.0 * before + 8.0 * after - after2) * (1.0 / 12.0) * living
        stacked(states * living, stack)
        first = dot(first_pick[part, :], stack[...], NN)
        second = dot(second_pick[part, :], stack[...], NN)
        rows_hi[...], rows_lo[...] = split2(first * second)
        cols_hi[:TAIL_QUADS, :], cols_lo[:TAIL_QUADS, :] = features(first_pick, second_pick, stack[...], ROWS_PAD + COLS, TAIL_QUADS)
        side = change[pl.ds(pl.multiple_of(x // 2 * TAIL_SIDES, TAIL_SIDES), TAIL_SIDES), :]
        cols_hi[TAIL_QUADS:, :], cols_lo[TAIL_QUADS:, :] = split2(side)
        total = product(rows_hi[...], rows_lo[...], cols_hi[...], cols_lo[...])
        tail[...] = total if step == 0 else tail[...] + total
    out[TAIL_AT:ENERGY_AT, :] = tail[...]


def with_tail(lengths, first_pick, second_pick, ends, mine, theirs, block):
    return pl.pallas_call(
        tail_kernel,
        out_shape=pltpu.VMEM((TILES, 128), jnp.float32),
        in_specs=[SMEM] + [VMEM] * 13,
        out_specs=VMEM,
        scratch_shapes=[
            pltpu.VMEM((4 * R, BLOCK), jnp.bfloat16),
            pltpu.VMEM((R, BLOCK), jnp.float32),
            pltpu.VMEM((128, BLOCK), jnp.bfloat16),
            pltpu.VMEM((128, BLOCK), jnp.bfloat16),
            pltpu.VMEM((TAIL_ROWS, BLOCK), jnp.bfloat16),
            pltpu.VMEM((TAIL_ROWS, BLOCK), jnp.bfloat16),
            pltpu.VMEM((TAIL_ROWS, 128), jnp.float32),
        ],
        input_output_aliases={13: 0},
        compiler_params=ROOM,
        name="tail",
    )(lengths, *[near_by(v) for v in (first_pick, second_pick, *ends, *mine, *theirs, block)])


def weights_of(lengths, energy):
    samples = lengths[0] - 4
    for k in range(1, TRAJ):
        samples += lengths[k] - 4
    samples = samples.astype(jnp.float32)
    inverse = (1.0 / UP) / jnp.sqrt(energy * (1.0 / (UP * UP)) / samples + 1e-06)
    high, middle, low = [part.astype(jnp.float32) for part in split3(inverse)]
    fill = jnp.where(lax.broadcasted_iota(jnp.int32, (8, R), 1) == 0, 1.0, 0.0)
    weights = jnp.concatenate([high, middle, low, fill], axis=1)
    tall = jnp.broadcast_to(weights[0:1, :], (128, 256)).astype(jnp.bfloat16)
    return samples, inverse, weights.astype(jnp.bfloat16), tall


def scale_kernel(lengths, first_pick, second_pick, block, out):
    x = lax.axis_index("x")
    samples, inverse, weights, tall = weights_of(lengths, block[ENERGY_AT : ENERGY_AT + 8, :R])
    by_row = dot(first_pick[:ROWS_PAD, :], tall, NT) * dot(second_pick[:ROWS_PAD, :], tall, NT) / samples
    by_column = (dot(weights, first_pick[ROWS_PAD:, :], NT) * dot(weights, second_pick[ROWS_PAD:, :], NT))[0:1, :]
    for k in range(COLS // 128):
        rows = slice(k * ROWS_PAD, (k + 1) * ROWS_PAD)
        out[rows, :] = block[rows, :] * by_row * by_column[:, k * 128 : (k + 1) * 128]
    sides = jnp.where(x < 2, inverse[0:1, :TAIL_SIDES], inverse[0:1, TAIL_SIDES:])
    column = jnp.concatenate([by_column[:, COLS:], sides], axis=1)
    tail_rows = jnp.where(x % 2 == 0, by_row[:TAIL_ROWS, :], by_row[128:, :])
    out[TAIL_AT:ENERGY_AT, :] = block[TAIL_AT:ENERGY_AT, :] * tail_rows * column


def scale(lengths, first_pick, second_pick, block):
    return pl.pallas_call(
        scale_kernel,
        out_shape=pltpu.VMEM((ENERGY_AT, 128), jnp.float32),
        in_specs=[SMEM, VMEM, VMEM, VMEM],
        out_specs=VMEM,
        compiler_params=ROOM,
        name="scale",
    )(lengths, *[near_by(v) for v in (first_pick, second_pick, block)])


def lay_kernel(own, left, right, far_top, far_bottom, gram_out, side_out, tails, sides):
    x = lax.axis_index("x")
    half = ENERGY_AT // 2

    def put(source, parts):
        for k in range(COLS // 128):
            first = k * ROWS_PAD
            lanes = pl.ds(pl.multiple_of((source * 4 + k) * 128, 128), 128)
            for part, low, high in parts:
                begin, end = max(first, low), min(first + ROWS, high)
                if begin < end:
                    gram_out[begin - first : end - first, lanes] = part[begin - low : end - low, :]
        for part, low, high in parts:
            begin, end = max(TAIL_AT, low), min(ENERGY_AT, high)
            if begin < end:
                tails[source, begin - TAIL_AT : end - TAIL_AT, :] = part[begin - low : end - low, :]

    put(x, [(own, 0, ENERGY_AT)])
    put((x + 3) % 4, [(left, 0, ENERGY_AT)])
    put((x + 1) % 4, [(right, 0, ENERGY_AT)])
    put((x + 2) % 4, [(far_top, 0, half), (far_bottom, half, ENERGY_AT)])
    sides[...] = jnp.zeros_like(sides)
    for x_of, low, high in ((0, 0, 128), (1, 128, ROWS)):
        count = high - low
        gram_out[low:high, 16 * 128 :] = tails[x_of, :count, :TAIL_QUADS]
        sides[low:high, :TAIL_SIDES] = tails[x_of, :count, TAIL_QUADS:]
        sides[low:high, TAIL_SIDES:R] = tails[x_of + 2, :count, TAIL_QUADS:]
    side_out[...] = sides[...].T[:R, :ROWS]


def lay(*pieces):
    return pl.pallas_call(
        lay_kernel,
        out_shape=(
            jax.ShapeDtypeStruct((ROWS, FEAT), jnp.float32),
            jax.ShapeDtypeStruct((R, ROWS), jnp.float32),
        ),
        in_specs=[VMEM] * 5,
        out_specs=(VMEM, VMEM),
        scratch_shapes=[pltpu.VMEM((4, TAIL_ROWS, 128), jnp.float32), pltpu.VMEM((384, 128), jnp.float32)],
        compiler_params=ROOM,
        name="lay",
    )(*[near_by(v) for v in pieces])


def ring(block):
    half = block.shape[0] // 2
    from_left, from_right = turn(block, "x", 1), turn(block, "x", 3)
    return block, from_left, from_right, turn(from_left[:half], "x", 1), turn(from_right[half:], "x", 3)


def shards(snapshots, basis, lengths):
    core = lax.axis_index("c")
    partial = jnp.einsum("cr,ct->rt", basis, snapshots, preferred_element_type=jnp.float32)
    mine = lax.dynamic_slice_in_dim(partial, core * HALF, HALF, 1)
    other = lax.dynamic_slice_in_dim(partial, (1 - core) * HALF, HALF, 1)
    half = mine + swap(other)
    message = (half + turn(half, "y", 2)) + (turn(half, "y", 1) + turn(half, "y", 3))
    first_pick, second_pick = picks()
    message, first_pick, second_pick = lax.optimization_barrier((message, first_pick, second_pick))
    mine = (message, turn(message, "x", 3), turn(message, "x", 2), turn(message, "x", 1))
    theirs = tuple(swap(part) for part in mine)
    edges = edges_of(mine)
    at = lambda c, z: c * 8 + z % 8
    same = lax.ppermute(edges, ("c", "z"), [(at(0, z), at(0, z + 7)) for z in range(8)] + [(at(1, z), at(1, z + 1)) for z in range(8)])
    cross = lax.ppermute(edges, ("c", "z"), [(at(0, z), at(1, z + 7)) for z in range(8)] + [(at(1, z), at(0, z + 1)) for z in range(8)])
    block = gram(lengths, first_pick, second_pick, mine, theirs)
    block = with_tail(lengths, first_pick, second_pick, (same, cross), mine, theirs, block)
    piece = jnp.sum(lax.all_to_all(block.reshape(8, PIECE, 128), "z", 0, 0, tiled=True), axis=0)
    block = everyone(piece, "z").reshape(TILES, 128)
    block = scale(lengths, first_pick, second_pick, block)
    gram_out, side_out = lay(*ring(block))
    return gram_out, side_out.T


def solution(mesh):
    grid = Mesh(mesh.devices.reshape(4, 2, 4, 8), ("y", "c", "x", "z"))
    return jax.shard_map(
        shards,
        mesh=grid,
        in_specs=(P(("y", "c"), ("x", "z")), P(("y", "c"), None), P()),
        out_specs=(P(("y", "c"), None), P(("y", "c"), None)),
        check_vma=False,
    )
```

```python
import functools

import jax
import jax.numpy as jnp
from jax import lax
from jax.experimental import pallas as pl
from jax.experimental.pallas import tpu as pltpu
from jax.sharding import Mesh, PartitionSpec as P


R = 64
FEAT = 2144
SLOT = 2048
TRAJ = 16
BLOCK = 1024
HALF = 512
ROWS = 268
ROWS_PAD = 272
COLS = 512
TAIL_QUADS = 96
TAIL_SIDES = 32
TAIL_ROWS = 144
TAIL_KEPT = 140
PICKS = ROWS_PAD + COLS + TAIL_QUADS
TAIL_AT = 4 * ROWS
PIECE = 152
EXTRA = 16
TILES = 8 * PIECE
OUT_TAIL = 4 * ROWS_PAD
OUT_ROWS = OUT_TAIL + TAIL_ROWS
UP = 2.0**16


def swap(value):
    return lax.ppermute(value, "c", [(0, 1), (1, 0)])


def turn(value, axis, by):
    count = lax.axis_size(axis)
    return lax.ppermute(value, axis, [(i, (i + by) % count) for i in range(count)])


def near_by(value):
    return pltpu.with_memory_space_constraint(value, pltpu.VMEM)


def everyone(value, axis):
    count = lax.axis_size(axis)
    spread = jnp.broadcast_to(value[None], (count,) + value.shape)
    return lax.all_to_all(spread, axis, 0, 0, tiled=True)


def one_hots(first_feature, count):
    lane = lax.broadcasted_iota(jnp.int32, (count, 256), 1)
    feature = lax.broadcasted_iota(jnp.int32, (count, 256), 0) + first_feature
    mode = lane & (R - 1)
    below = lane < 3 * R
    ends = R + (mode + 1) * R - (mode + 1) * mode // 2
    passed = jnp.where((lane < R) & (feature >= ends), 1.0, 0.0)
    row = jnp.sum(passed, axis=1, keepdims=True).astype(jnp.int32)
    start = R + row * R - row * (row - 1) // 2
    linear = feature < R
    first = jnp.where(linear, feature, row)
    second = jnp.where(linear, -1, feature - start + row)
    pick_first = below & (mode == first)
    pick_second = (below & (mode == second)) | (linear & (lane == 3 * R))
    as_type = lambda pick: jnp.where(pick, 1.0, 0.0).astype(jnp.bfloat16)
    return as_type(pick_first), as_type(pick_second)


def split3(value):
    high = value.astype(jnp.bfloat16)
    rest = value - high.astype(jnp.float32)
    middle = rest.astype(jnp.bfloat16)
    low = (rest - middle.astype(jnp.float32)).astype(jnp.bfloat16)
    return high, middle, low


def split2(value):
    high = value.astype(jnp.bfloat16)
    return high, (value - high.astype(jnp.float32)).astype(jnp.bfloat16)


def dot(left, right, dims):
    return lax.dot_general(left, right, (dims, ((), ())), preferred_element_type=jnp.float32)


NT = ((1,), (1,))
NN = ((1,), (0,))


def position():
    return lax.axis_index("c"), lax.axis_index("x"), lax.axis_index("z")


def pick_kernel(first_pick, second_pick):
    core, x, _ = position()
    space = lax.axis_index("y") * 2 + core
    for at, count, feature in (
        (0, ROWS_PAD, space * ROWS),
        (ROWS_PAD, COLS, x * COLS),
        (ROWS_PAD + COLS, TAIL_QUADS, 4 * COLS),
    ):
        first, second = one_hots(feature, count)
        first_pick[at : at + count, :] = first
        second_pick[at : at + count, :] = second


SMEM = pl.BlockSpec(memory_space=pltpu.SMEM)
VMEM = pl.BlockSpec(memory_space=pltpu.VMEM)
ROOM = pltpu.CompilerParams(vmem_limit_bytes=24 * 1024 * 1024)


def picks():
    return pl.pallas_call(
        pick_kernel,
        out_shape=(pltpu.VMEM((PICKS, 256), jnp.bfloat16), pltpu.VMEM((PICKS, 256), jnp.bfloat16)),
        out_specs=(VMEM, VMEM),
        compiler_params=ROOM,
        name="picks",
    )()


def whole_block(own, other, core):
    near = jnp.where(core == 0, own[...], other[...])
    far = jnp.where(core == 0, other[...], own[...])
    return jnp.concatenate([near, far], axis=1) * UP


def alive(lengths, start):
    lane = lax.broadcasted_iota(jnp.int32, (1, BLOCK), 1)
    one = lengths[(start + HALF) // SLOT % TRAJ]
    two = lengths[(start + 2 * HALF) // SLOT % TRAJ]
    offset = ((start + HALF) % SLOT + lane) & (SLOT - 1)
    limit = jnp.where(lane < HALF, one, two) - 3
    return jnp.where((offset >= 2) & (offset <= limit), 1.0, 0.0)


def features(first_pick, second_pick, stack, at, count):
    first = dot(first_pick[at : at + count, :], stack, NN)
    second = dot(second_pick[at : at + count, :], stack, NN)
    return split2(first * second)


def product(left_hi, left_lo, right_hi, right_lo):
    return dot(left_hi, right_hi, NT) + (dot(left_hi, right_lo, NT) + dot(left_lo, right_hi, NT))


def stacked(masked, stack):
    stack[:R, :], stack[R : 2 * R, :], stack[2 * R : 3 * R, :] = split3(masked)
    index = lax.broadcasted_iota(jnp.int32, masked.shape, 0)
    stack[3 * R :, :] = jnp.where(index == 0, 1.0, 0.0).astype(jnp.bfloat16)


def project_kernel(basis, snapshots, mine, other, basis_in, cells, total, arrived):
    core = lax.axis_index("c")
    parts = cells.shape[0]
    size = BLOCK // parts
    first = pltpu.make_async_copy(basis, basis_in, arrived.at[parts])
    loads = [
        pltpu.make_async_copy(snapshots.at[pl.ds(k * size, size), :], cells.at[k], arrived.at[k]) for k in range(parts)
    ]
    first.start()
    for load in loads:
        load.start()
    first.wait()
    for k, load in enumerate(loads):
        load.wait()
        part = dot(basis_in[:, k * size : (k + 1) * size], cells[k], NN)
        total[...] = part if k == 0 else total[...] + part
    low, high = total[:, :HALF], total[:, HALF:]
    mine[...] = jnp.where(core == 0, low, high)
    other[...] = jnp.where(core == 0, high, low)


def project(basis, snapshots):
    parts = 4
    return pl.pallas_call(
        project_kernel,
        out_shape=(pltpu.VMEM((R, HALF), jnp.float32), pltpu.VMEM((R, HALF), jnp.float32)),
        in_specs=[pl.BlockSpec(memory_space=pltpu.HBM)] * 2,
        out_specs=(VMEM, VMEM),
        scratch_shapes=[
            pltpu.VMEM((R, BLOCK), jnp.bfloat16),
            pltpu.VMEM((parts, BLOCK // parts, BLOCK), jnp.bfloat16),
            pltpu.VMEM((R, BLOCK), jnp.float32),
            pltpu.SemaphoreType.DMA((parts + 1,)),
        ],
        compiler_params=ROOM,
        name="project",
    )(*[pltpu.with_memory_space_constraint(v, pltpu.HBM) for v in (basis, snapshots)])


def stacked(masked, stack):
    stack[:R, :], stack[R : 2 * R, :], stack[2 * R : 3 * R, :] = split3(masked)
    index = lax.broadcasted_iota(jnp.int32, masked.shape, 0)
    stack[3 * R :, :] = jnp.where(index == 0, 1.0, 0.0).astype(jnp.bfloat16)


def add_blocks(lengths, first_pick, second_pick, steps, mine, theirs, sums, scratch, fresh):
    acc, tail, energy, ends = sums
    stack, change, rows_hi, rows_lo, cols_hi, cols_lo = scratch
    core, x, z = position()
    wide = lax.broadcasted_iota(jnp.int32, (R, BLOCK), 1)
    lane = lax.broadcasted_iota(jnp.int32, (R, 128), 1)
    part = pl.ds(pl.multiple_of(x % 2 * 128, 128), TAIL_ROWS)

    def add(ref, value, now, at=slice(None)):
        ref[:, at] = value if now else ref[:, at] + value

    for index, step in enumerate(steps):
        now = fresh and index == 0
        where = (x + step) % 4
        states = whole_block(mine[index], theirs[index], core)
        living = alive(lengths, (where * 8 + z) * BLOCK)
        before = jnp.where(wide < 1, 0.0, pltpu.roll(states, 1, 1))
        before2 = jnp.where(wide < 2, 0.0, pltpu.roll(states, 2, 1))
        after = jnp.where(wide >= BLOCK - 1, 0.0, pltpu.roll(states, BLOCK - 1, 1))
        after2 = jnp.where(wide >= BLOCK - 2, 0.0, pltpu.roll(states, BLOCK - 2, 1))
        change[...] = (before2 - 8.0 * before + 8.0 * after - after2) * (1.0 / 12.0) * living
        masked = states * living
        squares = masked * masked
        add(energy, functools.reduce(lambda a, b: a + b, [squares[:, k * 128 : (k + 1) * 128] for k in range(BLOCK // 128)]), now)
        four = states[:, 0:1]
        for e, at in ((1, 1), (2, BLOCK - 2), (3, BLOCK - 1)):
            four = jnp.where((lane & 3) == e, states[:, at : at + 1], four)
        ends[...] = jnp.where((lane >> 2) == where, four, jnp.zeros_like(four) if now else ends[...])
        stacked(masked, stack)
        rows_hi[...], rows_lo[...] = features(first_pick, second_pick, stack[...], 0, ROWS_PAD)
        for at in range(0, COLS, 256):
            right_hi, right_lo = features(first_pick, second_pick, stack[...], ROWS_PAD + at, 256)
            add(acc, product(rows_hi[...], rows_lo[...], right_hi, right_lo), now, slice(at, at + 256))
        cols_hi[:TAIL_QUADS, :], cols_lo[:TAIL_QUADS, :] = features(first_pick, second_pick, stack[...], ROWS_PAD + COLS, TAIL_QUADS)
        side = change[pl.ds(pl.multiple_of(x // 2 * TAIL_SIDES, TAIL_SIDES), TAIL_SIDES), :]
        cols_hi[TAIL_QUADS:, :], cols_lo[TAIL_QUADS:, :] = split2(side)
        add(tail, product(rows_hi[part, :], rows_lo[part, :], cols_hi[...], cols_lo[...]), now)


def gram_own_kernel(lengths, first_pick, second_pick, mine, theirs, *rest):
    add_blocks(lengths, first_pick, second_pick, (0,), (mine,), (theirs,), rest[:4], rest[4:], True)


def gram_rest_kernel(lengths, first_pick, second_pick, *rest):
    mine, theirs, given, (out, extra), sums, scratch = rest[:3], rest[3:6], rest[6:10], rest[10:12], rest[12:16], rest[16:]
    for ref, value in zip(sums, given):
        ref[...] = value[...]
    add_blocks(lengths, first_pick, second_pick, (1, 3, 2), mine, theirs, sums, scratch, False)
    acc, tail, energy, ends = sums
    for k in range(COLS // 128):
        out[k * ROWS : (k + 1) * ROWS, :] = acc[:ROWS, k * 128 : (k + 1) * 128]
    out[TAIL_AT : TAIL_AT + TAIL_KEPT, :] = tail[:TAIL_KEPT, :]
    out[TAIL_AT + TAIL_KEPT :, :] = jnp.zeros((TILES - TAIL_AT - TAIL_KEPT, 128), jnp.float32)
    total = lax.dot_general(
        jnp.ones((EXTRA, 128), jnp.float32),
        energy[...],
        (NT, ((), ())),
        precision=lax.Precision.HIGHEST,
        preferred_element_type=jnp.float32,
    )
    extra[...] = jnp.concatenate([ends[...].T[:EXTRA, :], total], axis=1)


SUMS = ((ROWS_PAD, COLS), (TAIL_ROWS, 128), (R, 128), (R, 128))
WORK = (
    pltpu.VMEM((4 * R, BLOCK), jnp.bfloat16),
    pltpu.VMEM((R, BLOCK), jnp.float32),
    pltpu.VMEM((ROWS_PAD, BLOCK), jnp.bfloat16),
    pltpu.VMEM((ROWS_PAD, BLOCK), jnp.bfloat16),
    pltpu.VMEM((128, BLOCK), jnp.bfloat16),
    pltpu.VMEM((128, BLOCK), jnp.bfloat16),
)


def gram(lengths, first_pick, second_pick, mine, theirs):
    own = pl.pallas_call(
        gram_own_kernel,
        out_shape=tuple(pltpu.VMEM(shape, jnp.float32) for shape in SUMS),
        in_specs=[SMEM] + [VMEM] * 4,
        out_specs=(VMEM,) * 4,
        scratch_shapes=WORK,
        compiler_params=ROOM,
        name="gram_own",
    )
    sums = own(lengths, *[near_by(v) for v in (first_pick, second_pick, mine[0], theirs[0])])
    order = (1, 3, 2)
    return pl.pallas_call(
        gram_rest_kernel,
        out_shape=(pltpu.VMEM((TILES, 128), jnp.float32), pltpu.VMEM((EXTRA, 128), jnp.float32)),
        in_specs=[SMEM] + [VMEM] * 12,
        out_specs=(VMEM, VMEM),
        scratch_shapes=tuple(pltpu.VMEM(shape, jnp.float32) for shape in SUMS) + WORK,
        compiler_params=ROOM,
        name="gram_rest",
    )(lengths, *[near_by(v) for v in (first_pick, second_pick, *[mine[k] for k in order], *[theirs[k] for k in order], *sums)])


def fold_kernel(parts, extra, out):
    out[:PIECE, :] = functools.reduce(lambda a, b: a + b, [parts[k] for k in range(8)])
    out[PIECE:, :] = extra[...]


def fold(parts, extra):
    return pl.pallas_call(
        fold_kernel,
        out_shape=pltpu.VMEM((PIECE + EXTRA, 128), jnp.float32),
        in_specs=[VMEM, VMEM],
        out_specs=VMEM,
        compiler_params=ROOM,
        name="fold",
    )(near_by(parts), near_by(extra))


def weights_of(lengths, energy):
    samples = lengths[0] - 4
    for k in range(1, TRAJ):
        samples += lengths[k] - 4
    samples = samples.astype(jnp.float32)
    inverse = (1.0 / UP) / jnp.sqrt(energy * (1.0 / (UP * UP)) / samples + 1e-06)
    high, middle, low = [part.astype(jnp.float32) for part in split3(inverse)]
    fill = jnp.where(lax.broadcasted_iota(jnp.int32, (8, R), 1) == 0, 1.0, 0.0)
    weights = jnp.concatenate([high, middle, low, fill], axis=1)
    tall = jnp.broadcast_to(weights[0:1, :], (128, 256)).astype(jnp.bfloat16)
    return samples, inverse, weights.astype(jnp.bfloat16), tall


def beyond_ends(lengths, first_pick, second_pick, parts, change):
    x = lax.axis_index("x")
    ends = jnp.concatenate([parts[k, PIECE:, :] for k in range(8)], axis=0).T[:R, :]
    lane = lax.broadcasted_iota(jnp.int32, (R, 128), 1)
    z, where, e = lane >> 4, (lane >> 2) & 3, lane & 3
    block = where * 8 + z
    before2 = jnp.where(z == 0, pltpu.roll(ends, 18, 1), pltpu.roll(ends, 14, 1))
    before = jnp.where(z == 0, pltpu.roll(ends, 17, 1), pltpu.roll(ends, 13, 1))
    after2 = jnp.where(z == 7, pltpu.roll(ends, 110, 1), pltpu.roll(ends, 114, 1))
    after = jnp.where(z == 7, pltpu.roll(ends, 111, 1), pltpu.roll(ends, 115, 1))
    left = jnp.where(block == 0, 0.0, jnp.where(e == 0, before2 - 8.0 * before, before2))
    right = jnp.where(block == 31, 0.0, jnp.where(e == 3, 8.0 * after - after2, -after2))
    time = block * BLOCK + jnp.where(e < 2, e, BLOCK - 4 + e) + HALF
    owner, offset = (time >> 11) & (TRAJ - 1), time & (SLOT - 1)
    limit = jnp.zeros_like(time)
    for k in range(TRAJ):
        limit = jnp.where(owner == k, lengths[k] - 3, limit)
    living = jnp.where((offset >= 2) & (offset <= limit), 1.0, 0.0)
    change[...] = jnp.where(e < 2, left, right) * (1.0 / 12.0) * living
    high, middle, low = [part.astype(jnp.float32) for part in split3(ends * living)]
    ones = jnp.where(lax.broadcasted_iota(jnp.int32, (R, 128), 0) == 0, 1.0, 0.0)
    stack = jnp.concatenate([high, middle, low, ones], axis=0).astype(jnp.bfloat16)
    part = pl.ds(pl.multiple_of(x % 2 * 128, 128), TAIL_ROWS)
    rows_hi, rows_lo = split2(dot(first_pick[part, :], stack, NN) * dot(second_pick[part, :], stack, NN))
    side = change[pl.ds(pl.multiple_of(x // 2 * TAIL_SIDES, TAIL_SIDES), TAIL_SIDES), :]
    cols_hi, cols_lo = split2(jnp.concatenate([jnp.zeros((TAIL_QUADS, 128), jnp.float32), side], axis=0))
    return product(rows_hi, rows_lo, cols_hi, cols_lo)


def scale_kernel(lengths, first_pick, second_pick, parts, out, change, row_weight, tail):
    x = lax.axis_index("x")
    energy = functools.reduce(lambda a, b: a + b, [parts[k, PIECE : PIECE + 8, R:] for k in range(8)])
    samples, inverse, weights, tall = weights_of(lengths, energy)
    row_weight[...] = dot(first_pick[:ROWS_PAD, :], tall, NT) * dot(second_pick[:ROWS_PAD, :], tall, NT) / samples
    by_column = (dot(weights, first_pick[ROWS_PAD:, :], NT) * dot(weights, second_pick[ROWS_PAD:, :], NT))[0:1, :]

    def pieces(begin, count):
        at = begin
        while at < begin + count:
            k, row = divmod(at, PIECE)
            size = min(PIECE - row, begin + count - at)
            yield at - begin, size, parts[k, row : row + size, :]
            at += size

    for k in range(COLS // 128):
        for at, size, part in pieces(k * ROWS, ROWS):
            to = k * ROWS_PAD + at
            out[to : to + size, :] = part * row_weight[at : at + size, :] * by_column[:, k * 128 : (k + 1) * 128]
    tail[...] = beyond_ends(lengths, first_pick, second_pick, parts, change)
    for at, size, part in pieces(TAIL_AT, TAIL_KEPT):
        tail[at : at + size, :] = tail[at : at + size, :] + part
    sides = jnp.where(x < 2, inverse[0:1, :TAIL_SIDES], inverse[0:1, TAIL_SIDES:])
    column = jnp.concatenate([by_column[:, COLS:], sides], axis=1)
    tail_rows = jnp.where(x % 2 == 0, row_weight[:TAIL_ROWS, :], row_weight[128:, :])
    out[OUT_TAIL:, :] = tail[...] * tail_rows * column
    for k in range(COLS // 128):
        out[k * ROWS_PAD + ROWS : (k + 1) * ROWS_PAD, :] = jnp.zeros((ROWS_PAD - ROWS, 128), jnp.float32)


def scale(lengths, first_pick, second_pick, parts):
    return pl.pallas_call(
        scale_kernel,
        out_shape=pltpu.VMEM((OUT_ROWS, 128), jnp.float32),
        in_specs=[SMEM, VMEM, VMEM, VMEM],
        out_specs=VMEM,
        scratch_shapes=[
            pltpu.VMEM((R, 128), jnp.float32),
            pltpu.VMEM((ROWS_PAD, 128), jnp.float32),
            pltpu.VMEM((TAIL_ROWS, 128), jnp.float32),
        ],
        compiler_params=ROOM,
        name="scale",
    )(lengths, *[near_by(v) for v in (first_pick, second_pick, parts)])


def lay_kernel(own, left, right, far_top, far_bottom, gram_out, side_out, tails, sides):
    x = lax.axis_index("x")
    half = OUT_ROWS // 2

    def put(source, parts):
        for k in range(COLS // 128):
            first = k * ROWS_PAD
            lanes = pl.ds(pl.multiple_of((source * 4 + k) * 128, 128), 128)
            for part, low, high in parts:
                begin, end = max(first, low), min(first + ROWS, high)
                if begin < end:
                    gram_out[begin - first : end - first, lanes] = part[begin - low : end - low, :]
        for part, low, high in parts:
            begin, end = max(OUT_TAIL, low), min(OUT_ROWS, high)
            if begin < end:
                tails[source, begin - OUT_TAIL : end - OUT_TAIL, :] = part[begin - low : end - low, :]

    put(x, [(own, 0, OUT_ROWS)])
    put((x + 3) % 4, [(left, 0, OUT_ROWS)])
    put((x + 1) % 4, [(right, 0, OUT_ROWS)])
    put((x + 2) % 4, [(far_top, 0, half), (far_bottom, half, OUT_ROWS)])
    sides[...] = jnp.zeros_like(sides)
    for x_of, low, high in ((0, 0, 128), (1, 128, ROWS)):
        count = high - low
        gram_out[low:high, 16 * 128 :] = tails[x_of, :count, :TAIL_QUADS]
        sides[low:high, :TAIL_SIDES] = tails[x_of, :count, TAIL_QUADS:]
        sides[low:high, TAIL_SIDES:R] = tails[x_of + 2, :count, TAIL_QUADS:]
    side_out[...] = sides[...].T[:R, :ROWS]


def lay(*pieces):
    return pl.pallas_call(
        lay_kernel,
        out_shape=(
            jax.ShapeDtypeStruct((ROWS, FEAT), jnp.float32),
            jax.ShapeDtypeStruct((R, ROWS), jnp.float32),
        ),
        in_specs=[VMEM] * 5,
        out_specs=(VMEM, VMEM),
        scratch_shapes=[pltpu.VMEM((4, TAIL_ROWS, 128), jnp.float32), pltpu.VMEM((384, 128), jnp.float32)],
        compiler_params=ROOM,
        name="lay",
    )(*[near_by(v) for v in pieces])


def ring(block):
    half = block.shape[0] // 2
    from_left, from_right = turn(block, "x", 1), turn(block, "x", 3)
    return block, from_left, from_right, turn(from_left[:half], "x", 1), turn(from_right[half:], "x", 3)


def shards(snapshots, basis, lengths):
    mine, other = project(basis.T, snapshots)
    half = mine + swap(other)
    message = (half + turn(half, "y", 2)) + (turn(half, "y", 1) + turn(half, "y", 3))
    first_pick, second_pick = picks()
    message, first_pick, second_pick = lax.optimization_barrier((message, first_pick, second_pick))
    across = turn(message, "x", 2)
    mine = (message, turn(message, "x", 3), across, turn(message, "x", 1))
    theirs = tuple(swap(part) for part in mine)
    block, extra = gram(lengths, first_pick, second_pick, mine, theirs)
    piece = fold(lax.all_to_all(block.reshape(8, PIECE, 128), "z", 0, 0, tiled=True), extra)
    parts = everyone(piece, "z").reshape(8, PIECE + EXTRA, 128)
    gram_out, side_out = lay(*ring(scale(lengths, first_pick, second_pick, parts)))
    return gram_out, side_out.T


def solution(mesh):
    grid = Mesh(mesh.devices.reshape(4, 2, 4, 8), ("y", "c", "x", "z"))
    return jax.shard_map(
        shards,
        mesh=grid,
        in_specs=(P(("y", "c"), ("x", "z")), P(("y", "c"), None), P()),
        out_specs=(P(("y", "c"), None), P(("y", "c"), None)),
        check_vma=False,
    )
```

```python
import functools

import jax
import jax.numpy as jnp
from jax import lax
from jax.experimental import pallas as pl
from jax.experimental.pallas import tpu as pltpu
from jax.sharding import Mesh, PartitionSpec as P


R = 64
FEAT = 2144
SLOT = 2048
TRAJ = 16
BLOCK = 1024
HALF = 512
ROWS = 268
ROWS_PAD = 272
COLS = 512
TAIL_QUADS = 96
TAIL_SIDES = 32
TAIL_ROWS = 144
TAIL_KEPT = 140
PICKS = ROWS_PAD + COLS + TAIL_QUADS
TAIL_AT = 4 * ROWS
PIECE = 152
EXTRA = 8
TILES = 8 * PIECE
ENERGY_AT = TAIL_AT + TAIL_KEPT
OUT_TAIL = 4 * ROWS_PAD
OUT_ROWS = OUT_TAIL + TAIL_ROWS
OUT_HALF = OUT_ROWS // 2
UP = 2.0**16


def swap(value):
    return lax.ppermute(value, "c", [(0, 1), (1, 0)])


def turn(value, axis, by):
    count = lax.axis_size(axis)
    return lax.ppermute(value, axis, [(i, (i + by) % count) for i in range(count)])


def near_by(value):
    return pltpu.with_memory_space_constraint(value, pltpu.VMEM)


def everyone(value, axis):
    count = lax.axis_size(axis)
    spread = jnp.broadcast_to(value[None], (count,) + value.shape)
    return lax.all_to_all(spread, axis, 0, 0, tiled=True)


def one_hots(first_feature, count):
    lane = lax.broadcasted_iota(jnp.int32, (count, 256), 1)
    feature = lax.broadcasted_iota(jnp.int32, (count, 256), 0) + first_feature
    mode = lane & (R - 1)
    below = lane < 3 * R
    ends = R + (mode + 1) * R - (mode + 1) * mode // 2
    passed = jnp.where((lane < R) & (feature >= ends), 1.0, 0.0)
    row = jnp.sum(passed, axis=1, keepdims=True).astype(jnp.int32)
    start = R + row * R - row * (row - 1) // 2
    linear = feature < R
    first = jnp.where(linear, feature, row)
    second = jnp.where(linear, -1, feature - start + row)
    pick_first = below & (mode == first)
    pick_second = (below & (mode == second)) | (linear & (lane == 3 * R))
    as_type = lambda pick: jnp.where(pick, 1.0, 0.0).astype(jnp.bfloat16)
    return as_type(pick_first), as_type(pick_second)


def split3(value):
    high = value.astype(jnp.bfloat16)
    rest = value - high.astype(jnp.float32)
    middle = rest.astype(jnp.bfloat16)
    low = (rest - middle.astype(jnp.float32)).astype(jnp.bfloat16)
    return high, middle, low


def split2(value):
    high = value.astype(jnp.bfloat16)
    return high, (value - high.astype(jnp.float32)).astype(jnp.bfloat16)


def dot(left, right, dims):
    return lax.dot_general(left, right, (dims, ((), ())), preferred_element_type=jnp.float32)


NT = ((1,), (1,))
NN = ((1,), (0,))


def position():
    return lax.axis_index("c"), lax.axis_index("x"), lax.axis_index("z")


def pick_kernel(first_pick, second_pick):
    core, x, _ = position()
    space = lax.axis_index("y") * 2 + core
    for at, count, feature in (
        (0, ROWS_PAD, space * ROWS),
        (ROWS_PAD, COLS, x * COLS),
        (ROWS_PAD + COLS, TAIL_QUADS, 4 * COLS),
    ):
        first, second = one_hots(feature, count)
        first_pick[at : at + count, :] = first
        second_pick[at : at + count, :] = second


SMEM = pl.BlockSpec(memory_space=pltpu.SMEM)
VMEM = pl.BlockSpec(memory_space=pltpu.VMEM)
ROOM = pltpu.CompilerParams(vmem_limit_bytes=24 * 1024 * 1024)


def picks():
    return pl.pallas_call(
        pick_kernel,
        out_shape=(pltpu.VMEM((PICKS, 256), jnp.bfloat16), pltpu.VMEM((PICKS, 256), jnp.bfloat16)),
        out_specs=(VMEM, VMEM),
        compiler_params=ROOM,
        name="picks",
    )()


def whole_block(own, other, core):
    near = jnp.where(core == 0, own[...], other[...])
    far = jnp.where(core == 0, other[...], own[...])
    return jnp.concatenate([near, far], axis=1) * UP


def alive(lengths, start):
    lane = lax.broadcasted_iota(jnp.int32, (1, BLOCK), 1)
    one = lengths[(start + HALF) // SLOT % TRAJ]
    two = lengths[(start + 2 * HALF) // SLOT % TRAJ]
    offset = ((start + HALF) % SLOT + lane) & (SLOT - 1)
    limit = jnp.where(lane < HALF, one, two) - 3
    return jnp.where((offset >= 2) & (offset <= limit), 1.0, 0.0)


def features(first_pick, second_pick, stack, at, count):
    first = dot(first_pick[at : at + count, :], stack, NN)
    second = dot(second_pick[at : at + count, :], stack, NN)
    return split2(first * second)


def product(left_hi, left_lo, right_hi, right_lo):
    return dot(left_hi, right_hi, NT) + (dot(left_hi, right_lo, NT) + dot(left_lo, right_hi, NT))


def stacked(masked, stack):
    stack[:R, :], stack[R : 2 * R, :], stack[2 * R : 3 * R, :] = split3(masked)
    index = lax.broadcasted_iota(jnp.int32, masked.shape, 0)
    stack[3 * R :, :] = jnp.where(index == 0, 1.0, 0.0).astype(jnp.bfloat16)


def project_kernel(basis, snapshots, mine, other, basis_in, cells, total, arrived):
    core = lax.axis_index("c")
    parts = cells.shape[0]
    size = BLOCK // parts
    first = pltpu.make_async_copy(basis, basis_in, arrived.at[parts])
    loads = [
        pltpu.make_async_copy(snapshots.at[pl.ds(k * size, size), :], cells.at[k], arrived.at[k]) for k in range(parts)
    ]
    first.start()
    for load in loads:
        load.start()
    first.wait()
    for k, load in enumerate(loads):
        load.wait()
        part = dot(basis_in[:, k * size : (k + 1) * size], cells[k], NN)
        total[...] = part if k == 0 else total[...] + part
    low, high = total[:, :HALF], total[:, HALF:]
    mine[...] = jnp.where(core == 0, low, high)
    other[...] = jnp.where(core == 0, high, low)


def project(basis, snapshots):
    parts = 4
    return pl.pallas_call(
        project_kernel,
        out_shape=(pltpu.VMEM((R, HALF), jnp.float32), pltpu.VMEM((R, HALF), jnp.float32)),
        in_specs=[pl.BlockSpec(memory_space=pltpu.HBM)] * 2,
        out_specs=(VMEM, VMEM),
        scratch_shapes=[
            pltpu.VMEM((R, BLOCK), jnp.bfloat16),
            pltpu.VMEM((parts, BLOCK // parts, BLOCK), jnp.bfloat16),
            pltpu.VMEM((R, BLOCK), jnp.float32),
            pltpu.SemaphoreType.DMA((parts + 1,)),
        ],
        compiler_params=ROOM,
        name="project",
    )(*[pltpu.with_memory_space_constraint(v, pltpu.HBM) for v in (basis, snapshots)])


def stacked(masked, stack):
    stack[:R, :], stack[R : 2 * R, :], stack[2 * R : 3 * R, :] = split3(masked)
    index = lax.broadcasted_iota(jnp.int32, masked.shape, 0)
    stack[3 * R :, :] = jnp.where(index == 0, 1.0, 0.0).astype(jnp.bfloat16)


def add_blocks(lengths, first_pick, second_pick, steps, mine, theirs, sums, scratch, fresh, out=None):
    acc, tail, energy, ends = sums
    stack, change, rows_hi, rows_lo, cols_hi, cols_lo = scratch
    core, x, z = position()
    wide = lax.broadcasted_iota(jnp.int32, (R, BLOCK), 1)
    lane = lax.broadcasted_iota(jnp.int32, (R, 128), 1)
    part = pl.ds(pl.multiple_of(x % 2 * 128, 128), TAIL_ROWS)

    def add(ref, value, now, at=slice(None)):
        ref[:, at] = value if now else ref[:, at] + value

    for index, step in enumerate(steps):
        now = fresh and index == 0
        where = (x + step) % 4
        states = whole_block(mine[index], theirs[index], core)
        living = alive(lengths, (where * 8 + z) * BLOCK)
        before = jnp.where(wide < 1, 0.0, pltpu.roll(states, 1, 1))
        before2 = jnp.where(wide < 2, 0.0, pltpu.roll(states, 2, 1))
        after = jnp.where(wide >= BLOCK - 1, 0.0, pltpu.roll(states, BLOCK - 1, 1))
        after2 = jnp.where(wide >= BLOCK - 2, 0.0, pltpu.roll(states, BLOCK - 2, 1))
        change[...] = (before2 - 8.0 * before + 8.0 * after - after2) * (1.0 / 12.0) * living
        masked = states * living
        squares = masked * masked
        add(energy, functools.reduce(lambda a, b: a + b, [squares[:, k * 128 : (k + 1) * 128] for k in range(BLOCK // 128)]), now)
        four = states[:, 0:1]
        for e, at in ((1, 1), (2, BLOCK - 2), (3, BLOCK - 1)):
            four = jnp.where((lane & 3) == e, states[:, at : at + 1], four)
        ends[...] = jnp.where((lane >> 2) == where, four, jnp.zeros_like(four) if now else ends[...])
        stacked(masked, stack)
        rows_hi[...], rows_lo[...] = features(first_pick, second_pick, stack[...], 0, ROWS_PAD)
        for at in range(0, COLS, 256):
            right_hi, right_lo = features(first_pick, second_pick, stack[...], ROWS_PAD + at, 256)
            value = product(rows_hi[...], rows_lo[...], right_hi, right_lo)
            if out is None:
                add(acc, value, now, slice(at, at + 256))
                continue
            value = acc[:, at : at + 256] + value
            for k in range(at // 128, at // 128 + 2):
                out[k * ROWS : (k + 1) * ROWS, :] = value[:ROWS, k * 128 - at : (k + 1) * 128 - at]
        cols_hi[:TAIL_QUADS, :], cols_lo[:TAIL_QUADS, :] = features(first_pick, second_pick, stack[...], ROWS_PAD + COLS, TAIL_QUADS)
        side = change[pl.ds(pl.multiple_of(x // 2 * TAIL_SIDES, TAIL_SIDES), TAIL_SIDES), :]
        cols_hi[TAIL_QUADS:, :], cols_lo[TAIL_QUADS:, :] = split2(side)
        add(tail, product(rows_hi[part, :], rows_lo[part, :], cols_hi[...], cols_lo[...]), now)


def gram_own_kernel(lengths, first_pick, second_pick, mine, theirs, *rest):
    add_blocks(lengths, first_pick, second_pick, (0,), (mine,), (theirs,), rest[:4], rest[4:], True)


def gram_beside_kernel(lengths, first_pick, second_pick, *rest):
    mine, theirs, sums, scratch = rest[:2], rest[2:4], rest[8:12], rest[12:]
    add_blocks(lengths, first_pick, second_pick, (1, 3), mine, theirs, sums, scratch, False)


def gram_across_kernel(lengths, first_pick, second_pick, *rest):
    mine, theirs, given, (out, extra), more, scratch = rest[:1], rest[1:2], rest[2:6], rest[6:8], rest[8:11], rest[11:]
    for ref, value in zip(more, given[1:]):
        ref[...] = value[...]
    sums = (given[0], *more)
    add_blocks(lengths, first_pick, second_pick, (2,), mine, theirs, sums, scratch, False, out)
    _, tail, energy, ends = sums
    out[TAIL_AT : TAIL_AT + TAIL_KEPT, :] = tail[:TAIL_KEPT, :]
    total = lax.dot_general(
        jnp.ones((8, 128), jnp.float32),
        energy[...],
        (NT, ((), ())),
        precision=lax.Precision.HIGHEST,
        preferred_element_type=jnp.float32,
    )
    out[ENERGY_AT:, :] = jnp.concatenate([total, jnp.zeros_like(total)], axis=1)[: TILES - ENERGY_AT, :]
    flat = ends[...].T
    extra[...] = jnp.concatenate([flat[:EXTRA, :], flat[EXTRA : 2 * EXTRA, :]], axis=1)


SUMS = ((ROWS_PAD, COLS), (TAIL_ROWS, 128), (R, 128), (R, 128))
WORK = (
    pltpu.VMEM((4 * R, BLOCK), jnp.bfloat16),
    pltpu.VMEM((R, BLOCK), jnp.float32),
    pltpu.VMEM((ROWS_PAD, BLOCK), jnp.bfloat16),
    pltpu.VMEM((ROWS_PAD, BLOCK), jnp.bfloat16),
    pltpu.VMEM((128, BLOCK), jnp.bfloat16),
    pltpu.VMEM((128, BLOCK), jnp.bfloat16),
)


def gram(lengths, first_pick, second_pick, mine, theirs):
    shapes = tuple(pltpu.VMEM(shape, jnp.float32) for shape in SUMS)
    own = pl.pallas_call(
        gram_own_kernel,
        out_shape=shapes,
        in_specs=[SMEM] + [VMEM] * 4,
        out_specs=(VMEM,) * 4,
        scratch_shapes=WORK,
        compiler_params=ROOM,
        name="gram_own",
    )
    beside = pl.pallas_call(
        gram_beside_kernel,
        out_shape=shapes,
        in_specs=[SMEM] + [VMEM] * 10,
        out_specs=(VMEM,) * 4,
        scratch_shapes=WORK,
        input_output_aliases={7 + k: k for k in range(4)},
        compiler_params=ROOM,
        name="gram_beside",
    )
    across = pl.pallas_call(
        gram_across_kernel,
        out_shape=(pltpu.VMEM((TILES, 128), jnp.float32), pltpu.VMEM((EXTRA, 128), jnp.float32)),
        in_specs=[SMEM] + [VMEM] * 8,
        out_specs=(VMEM, VMEM),
        scratch_shapes=tuple(pltpu.VMEM(shape, jnp.float32) for shape in SUMS[1:]) + WORK,
        compiler_params=ROOM,
        name="gram_across",
    )
    kept = [near_by(v) for v in (first_pick, second_pick)]
    sums = own(lengths, *kept, near_by(mine[0]), near_by(theirs[0]))
    sums = beside(lengths, *kept, *[near_by(v) for v in (mine[1], mine[3], theirs[1], theirs[3], *sums)])
    return across(lengths, *kept, *[near_by(v) for v in (mine[2], theirs[2], *sums)])


def fold_kernel(parts, extra, out):
    out[:PIECE, :] = functools.reduce(lambda a, b: a + b, [parts[k] for k in range(8)])
    out[PIECE:, :] = extra[...]


def fold(parts, extra):
    return pl.pallas_call(
        fold_kernel,
        out_shape=pltpu.VMEM((PIECE + EXTRA, 128), jnp.float32),
        in_specs=[VMEM, VMEM],
        out_specs=VMEM,
        compiler_params=ROOM,
        name="fold",
    )(near_by(parts), near_by(extra))


def weights_of(lengths, energy):
    samples = lengths[0] - 4
    for k in range(1, TRAJ):
        samples += lengths[k] - 4
    samples = samples.astype(jnp.float32)
    inverse = (1.0 / UP) / jnp.sqrt(energy * (1.0 / (UP * UP)) / samples + 1e-06)
    high, middle, low = [part.astype(jnp.float32) for part in split3(inverse)]
    fill = jnp.where(lax.broadcasted_iota(jnp.int32, (8, R), 1) == 0, 1.0, 0.0)
    weights = jnp.concatenate([high, middle, low, fill], axis=1)
    tall = jnp.broadcast_to(weights[0:1, :], (128, 256)).astype(jnp.bfloat16)
    return samples, inverse, weights.astype(jnp.bfloat16), tall


def beyond_ends(lengths, first_pick, second_pick, parts, change):
    x = lax.axis_index("x")
    flat = [parts[k, PIECE:, at : at + R] for k in range(8) for at in (0, R)]
    flat = jnp.concatenate(flat, axis=0)
    ends = jnp.concatenate([flat, flat], axis=1).T[:R, :]
    lane = lax.broadcasted_iota(jnp.int32, (R, 128), 1)
    z, where, e = lane >> 4, (lane >> 2) & 3, lane & 3
    block = where * 8 + z
    before2 = jnp.where(z == 0, pltpu.roll(ends, 18, 1), pltpu.roll(ends, 14, 1))
    before = jnp.where(z == 0, pltpu.roll(ends, 17, 1), pltpu.roll(ends, 13, 1))
    after2 = jnp.where(z == 7, pltpu.roll(ends, 110, 1), pltpu.roll(ends, 114, 1))
    after = jnp.where(z == 7, pltpu.roll(ends, 111, 1), pltpu.roll(ends, 115, 1))
    left = jnp.where(block == 0, 0.0, jnp.where(e == 0, before2 - 8.0 * before, before2))
    right = jnp.where(block == 31, 0.0, jnp.where(e == 3, 8.0 * after - after2, -after2))
    time = block * BLOCK + jnp.where(e < 2, e, BLOCK - 4 + e) + HALF
    owner, offset = (time >> 11) & (TRAJ - 1), time & (SLOT - 1)
    limit = jnp.zeros_like(time)
    for k in range(TRAJ):
        limit = jnp.where(owner == k, lengths[k] - 3, limit)
    living = jnp.where((offset >= 2) & (offset <= limit), 1.0, 0.0)
    change[...] = jnp.where(e < 2, left, right) * (1.0 / 12.0) * living
    high, middle, low = [part.astype(jnp.float32) for part in split3(ends * living)]
    ones = jnp.where(lax.broadcasted_iota(jnp.int32, (R, 128), 0) == 0, 1.0, 0.0)
    stack = jnp.concatenate([high, middle, low, ones], axis=0).astype(jnp.bfloat16)
    part = pl.ds(pl.multiple_of(x % 2 * 128, 128), TAIL_ROWS)
    rows_hi, rows_lo = split2(dot(first_pick[part, :], stack, NN) * dot(second_pick[part, :], stack, NN))
    side = change[pl.ds(pl.multiple_of(x // 2 * TAIL_SIDES, TAIL_SIDES), TAIL_SIDES), :]
    cols_hi, cols_lo = split2(jnp.concatenate([jnp.zeros((TAIL_QUADS, 128), jnp.float32), side], axis=0))
    return product(rows_hi, rows_lo, cols_hi, cols_lo)


def scale_kernel(lengths, first_pick, second_pick, parts, top, bottom, change, row_weight, tail):
    x = lax.axis_index("x")

    def put(at, value):
        cut = min(max(OUT_HALF - at, 0), value.shape[0])
        if cut:
            top[at : at + cut, :] = value[:cut, :]
        if cut < value.shape[0]:
            bottom[at + cut - OUT_HALF : at + value.shape[0] - OUT_HALF, :] = value[cut:, :]

    at = ENERGY_AT - 7 * PIECE
    energy = jnp.broadcast_to(parts[7, at : at + 1, :R], (8, R))
    samples, inverse, weights, tall = weights_of(lengths, energy)
    row_weight[...] = dot(first_pick[:ROWS_PAD, :], tall, NT) * dot(second_pick[:ROWS_PAD, :], tall, NT) / samples
    by_column = (dot(weights, first_pick[ROWS_PAD:, :], NT) * dot(weights, second_pick[ROWS_PAD:, :], NT))[0:1, :]

    def pieces(begin, count):
        at = begin
        while at < begin + count:
            k, row = divmod(at, PIECE)
            size = min(PIECE - row, begin + count - at)
            yield at - begin, size, parts[k, row : row + size, :]
            at += size

    for k in range(COLS // 128):
        for at, size, part in pieces(k * ROWS, ROWS):
            put(k * ROWS_PAD + at, part * row_weight[at : at + size, :] * by_column[:, k * 128 : (k + 1) * 128])
    tail[...] = beyond_ends(lengths, first_pick, second_pick, parts, change)
    for at, size, part in pieces(TAIL_AT, TAIL_KEPT):
        tail[at : at + size, :] = tail[at : at + size, :] + part
    sides = jnp.where(x < 2, inverse[0:1, :TAIL_SIDES], inverse[0:1, TAIL_SIDES:])
    column = jnp.concatenate([by_column[:, COLS:], sides], axis=1)
    tail_rows = jnp.where(x % 2 == 0, row_weight[:TAIL_ROWS, :], row_weight[128:, :])
    put(OUT_TAIL, tail[...] * tail_rows * column)
    for k in range(COLS // 128):
        put(k * ROWS_PAD + ROWS, jnp.zeros((ROWS_PAD - ROWS, 128), jnp.float32))


def scale(lengths, first_pick, second_pick, parts):
    return pl.pallas_call(
        scale_kernel,
        out_shape=(pltpu.VMEM((OUT_HALF, 128), jnp.float32), pltpu.VMEM((OUT_HALF, 128), jnp.float32)),
        in_specs=[SMEM, VMEM, VMEM, VMEM],
        out_specs=(VMEM, VMEM),
        scratch_shapes=[
            pltpu.VMEM((R, 128), jnp.float32),
            pltpu.VMEM((ROWS_PAD, 128), jnp.float32),
            pltpu.VMEM((TAIL_ROWS, 128), jnp.float32),
        ],
        compiler_params=ROOM,
        name="scale",
    )(lengths, *[near_by(v) for v in (first_pick, second_pick, parts)])


def lay_kernel(*refs):
    pieces, (gram_out, side_out, tails, sides) = refs[:8], refs[8:]
    x = lax.axis_index("x")

    def put(source, parts):
        for k in range(COLS // 128):
            first = k * ROWS_PAD
            lanes = pl.ds(pl.multiple_of((source * 4 + k) * 128, 128), 128)
            for part, low, high in parts:
                begin, end = max(first, low), min(first + ROWS, high)
                if begin < end:
                    gram_out[begin - first : end - first, lanes] = part[begin - low : end - low, :]
        for part, low, high in parts:
            begin, end = max(OUT_TAIL, low), min(OUT_ROWS, high)
            if begin < end:
                tails[source, begin - OUT_TAIL : end - OUT_TAIL, :] = part[begin - low : end - low, :]

    for by, top, bottom in zip((0, 3, 1, 2), pieces[::2], pieces[1::2]):
        put((x + by) % 4, [(top, 0, OUT_HALF), (bottom, OUT_HALF, OUT_ROWS)])
    sides[...] = jnp.zeros_like(sides)
    for x_of, low, high in ((0, 0, 128), (1, 128, ROWS)):
        count = high - low
        gram_out[low:high, 16 * 128 :] = tails[x_of, :count, :TAIL_QUADS]
        sides[low:high, :TAIL_SIDES] = tails[x_of, :count, TAIL_QUADS:]
        sides[low:high, TAIL_SIDES:R] = tails[x_of + 2, :count, TAIL_QUADS:]
    side_out[...] = sides[...].T[:R, :ROWS]


def lay(*pieces):
    return pl.pallas_call(
        lay_kernel,
        out_shape=(
            jax.ShapeDtypeStruct((ROWS, FEAT), jnp.float32),
            jax.ShapeDtypeStruct((R, ROWS), jnp.float32),
        ),
        in_specs=[VMEM] * 8,
        out_specs=(VMEM, VMEM),
        scratch_shapes=[pltpu.VMEM((4, TAIL_ROWS, 128), jnp.float32), pltpu.VMEM((384, 128), jnp.float32)],
        compiler_params=ROOM,
        name="lay",
    )(*[near_by(v) for v in pieces])


def ring(top, bottom):
    left_top, right_bottom = turn(top, "x", 1), turn(bottom, "x", 3)
    left_bottom, right_top = turn(bottom, "x", 1), turn(top, "x", 3)
    far_top, far_bottom = turn(left_top, "x", 1), turn(right_bottom, "x", 3)
    return top, bottom, left_top, left_bottom, right_top, right_bottom, far_top, far_bottom


def shards(snapshots, basis, lengths):
    mine, other = project(basis.T, snapshots)
    half = mine + swap(other)
    message = (half + turn(half, "y", 2)) + (turn(half, "y", 1) + turn(half, "y", 3))
    first_pick, second_pick = picks()
    message, first_pick, second_pick = lax.optimization_barrier((message, first_pick, second_pick))
    across = turn(message, "x", 2)
    mine = (message, turn(message, "x", 3), across, turn(message, "x", 1))
    theirs = tuple(swap(part) for part in (mine[0], mine[1], mine[3]))
    theirs = (*theirs[:2], swap(across), theirs[2])
    block, extra = gram(lengths, first_pick, second_pick, mine, theirs)
    piece = fold(lax.all_to_all(block.reshape(8, PIECE, 128), "z", 0, 0, tiled=True), extra)
    parts = everyone(piece, "z").reshape(8, PIECE + EXTRA, 128)
    gram_out, side_out = lay(*ring(*scale(lengths, first_pick, second_pick, parts)))
    return gram_out, side_out.T


def solution(mesh):
    grid = Mesh(mesh.devices.reshape(4, 2, 4, 8), ("y", "c", "x", "z"))
    return jax.shard_map(
        shards,
        mesh=grid,
        in_specs=(P(("y", "c"), ("x", "z")), P(("y", "c"), None), P()),
        out_specs=(P(("y", "c"), None), P(("y", "c"), None)),
        check_vma=False,
    )
```

```python
import functools

import jax
import jax.numpy as jnp
from jax import lax
from jax.experimental import pallas as pl
from jax.experimental.pallas import tpu as pltpu
from jax.sharding import Mesh, PartitionSpec as P


R = 64
FEAT = 2144
SLOT = 2048
TRAJ = 16
BLOCK = 1024
HALF = 512
ROWS = 268
ROWS_PAD = 272
COLS = 512
TAIL_QUADS = 96
TAIL_SIDES = 32
TAIL_ROWS = 144
TAIL_KEPT = 140
PICKS = ROWS_PAD + COLS + TAIL_QUADS
TAIL_AT = 4 * ROWS
PIECE = 152
EXTRA = 8
TILES = 8 * PIECE
ENERGY_AT = TAIL_AT + TAIL_KEPT
OUT_TAIL = 4 * ROWS_PAD
OUT_ROWS = OUT_TAIL + TAIL_ROWS
OUT_HALF = OUT_ROWS // 2
UP = 2.0**16


def swap(value):
    return lax.ppermute(value, "c", [(0, 1), (1, 0)])


def turn(value, axis, by):
    count = lax.axis_size(axis)
    return lax.ppermute(value, axis, [(i, (i + by) % count) for i in range(count)])


def near_by(value):
    return pltpu.with_memory_space_constraint(value, pltpu.VMEM)


def everyone(value, axis):
    count = lax.axis_size(axis)
    spread = jnp.broadcast_to(value[None], (count,) + value.shape)
    return lax.all_to_all(spread, axis, 0, 0, tiled=True)


def one_hots(first_feature, count):
    lane = lax.broadcasted_iota(jnp.int32, (count, 256), 1)
    feature = lax.broadcasted_iota(jnp.int32, (count, 256), 0) + first_feature
    mode = lane & (R - 1)
    below = lane < 3 * R
    ends = R + (mode + 1) * R - (mode + 1) * mode // 2
    passed = jnp.where((lane < R) & (feature >= ends), 1.0, 0.0)
    row = jnp.sum(passed, axis=1, keepdims=True).astype(jnp.int32)
    start = R + row * R - row * (row - 1) // 2
    linear = feature < R
    first = jnp.where(linear, feature, row)
    second = jnp.where(linear, -1, feature - start + row)
    pick_first = below & (mode == first)
    pick_second = (below & (mode == second)) | (linear & (lane == 3 * R))
    as_type = lambda pick: jnp.where(pick, 1.0, 0.0).astype(jnp.bfloat16)
    return as_type(pick_first), as_type(pick_second)


def split3(value):
    high = value.astype(jnp.bfloat16)
    rest = value - high.astype(jnp.float32)
    middle = rest.astype(jnp.bfloat16)
    low = (rest - middle.astype(jnp.float32)).astype(jnp.bfloat16)
    return high, middle, low


def split2(value):
    high = value.astype(jnp.bfloat16)
    return high, (value - high.astype(jnp.float32)).astype(jnp.bfloat16)


def dot(left, right, dims):
    return lax.dot_general(left, right, (dims, ((), ())), preferred_element_type=jnp.float32)


NT = ((1,), (1,))
NN = ((1,), (0,))


def position():
    return lax.axis_index("c"), lax.axis_index("x"), lax.axis_index("z")


def pick_kernel(first_pick, second_pick):
    core, x, _ = position()
    space = lax.axis_index("y") * 2 + core
    for at, count, feature in (
        (0, ROWS_PAD, space * ROWS),
        (ROWS_PAD, COLS, x * COLS),
        (ROWS_PAD + COLS, TAIL_QUADS, 4 * COLS),
    ):
        first, second = one_hots(feature, count)
        first_pick[at : at + count, :] = first
        second_pick[at : at + count, :] = second


SMEM = pl.BlockSpec(memory_space=pltpu.SMEM)
VMEM = pl.BlockSpec(memory_space=pltpu.VMEM)
ROOM = pltpu.CompilerParams(vmem_limit_bytes=24 * 1024 * 1024)


def picks():
    return pl.pallas_call(
        pick_kernel,
        out_shape=(pltpu.VMEM((PICKS, 256), jnp.bfloat16), pltpu.VMEM((PICKS, 256), jnp.bfloat16)),
        out_specs=(VMEM, VMEM),
        compiler_params=ROOM,
        name="picks",
    )()


def whole_block(own, other, core):
    near = jnp.where(core == 0, own[...], other[...])
    far = jnp.where(core == 0, other[...], own[...])
    return jnp.concatenate([near, far], axis=1) * UP


def alive(lengths, start):
    lane = lax.broadcasted_iota(jnp.int32, (1, BLOCK), 1)
    one = lengths[(start + HALF) // SLOT % TRAJ]
    two = lengths[(start + 2 * HALF) // SLOT % TRAJ]
    offset = ((start + HALF) % SLOT + lane) & (SLOT - 1)
    limit = jnp.where(lane < HALF, one, two) - 3
    return jnp.where((offset >= 2) & (offset <= limit), 1.0, 0.0)


def features(first_pick, second_pick, stack, at, count):
    first = dot(first_pick[at : at + count, :], stack, NN)
    second = dot(second_pick[at : at + count, :], stack, NN)
    return split2(first * second)


def product(left_hi, left_lo, right_hi, right_lo):
    return dot(left_hi, right_hi, NT) + dot(left_lo, right_hi, NT) + dot(left_hi, right_lo, NT)


def stacked(masked, stack):
    stack[:R, :], stack[R : 2 * R, :], stack[2 * R : 3 * R, :] = split3(masked)
    index = lax.broadcasted_iota(jnp.int32, masked.shape, 0)
    stack[3 * R :, :] = jnp.where(index == 0, 1.0, 0.0).astype(jnp.bfloat16)


def project_kernel(basis, snapshots, mine, other, basis_in, cells, total, arrived):
    core = lax.axis_index("c")
    parts = cells.shape[0]
    size = BLOCK // parts
    first = pltpu.make_async_copy(basis, basis_in, arrived.at[parts])
    loads = [
        pltpu.make_async_copy(snapshots.at[pl.ds(k * size, size), :], cells.at[k], arrived.at[k]) for k in range(parts)
    ]
    first.start()
    for load in loads:
        load.start()
    first.wait()
    for k, load in enumerate(loads):
        load.wait()
        part = dot(basis_in[:, k * size : (k + 1) * size], cells[k], NN)
        total[...] = part if k == 0 else total[...] + part
    low, high = total[:, :HALF], total[:, HALF:]
    mine[...] = jnp.where(core == 0, low, high)
    other[...] = jnp.where(core == 0, high, low)


def project(basis, snapshots):
    parts = 4
    return pl.pallas_call(
        project_kernel,
        out_shape=(pltpu.VMEM((R, HALF), jnp.float32), pltpu.VMEM((R, HALF), jnp.float32)),
        in_specs=[pl.BlockSpec(memory_space=pltpu.HBM)] * 2,
        out_specs=(VMEM, VMEM),
        scratch_shapes=[
            pltpu.VMEM((R, BLOCK), jnp.bfloat16),
            pltpu.VMEM((parts, BLOCK // parts, BLOCK), jnp.bfloat16),
            pltpu.VMEM((R, BLOCK), jnp.float32),
            pltpu.SemaphoreType.DMA((parts + 1,)),
        ],
        compiler_params=ROOM,
        name="project",
    )(*[pltpu.with_memory_space_constraint(v, pltpu.HBM) for v in (basis, snapshots)])


def stacked(masked, stack):
    stack[:R, :], stack[R : 2 * R, :], stack[2 * R : 3 * R, :] = split3(masked)
    index = lax.broadcasted_iota(jnp.int32, masked.shape, 0)
    stack[3 * R :, :] = jnp.where(index == 0, 1.0, 0.0).astype(jnp.bfloat16)


def add_blocks(lengths, first_pick, second_pick, steps, mine, theirs, sums, scratch, fresh, out=None):
    acc, tail, energy, ends = sums
    stack, change, rows_hi, rows_lo, cols_hi, cols_lo = scratch
    core, x, z = position()
    wide = lax.broadcasted_iota(jnp.int32, (R, BLOCK), 1)
    lane = lax.broadcasted_iota(jnp.int32, (R, 128), 1)
    part = pl.ds(pl.multiple_of(x % 2 * 128, 128), TAIL_ROWS)

    def add(ref, value, now, at=slice(None)):
        ref[:, at] = value if now else ref[:, at] + value

    for index, step in enumerate(steps):
        now = fresh and index == 0
        where = (x + step) % 4
        states = whole_block(mine[index], theirs[index], core)
        living = alive(lengths, (where * 8 + z) * BLOCK)
        before = jnp.where(wide < 1, 0.0, pltpu.roll(states, 1, 1))
        before2 = jnp.where(wide < 2, 0.0, pltpu.roll(states, 2, 1))
        after = jnp.where(wide >= BLOCK - 1, 0.0, pltpu.roll(states, BLOCK - 1, 1))
        after2 = jnp.where(wide >= BLOCK - 2, 0.0, pltpu.roll(states, BLOCK - 2, 1))
        change[...] = (before2 - 8.0 * before + 8.0 * after - after2) * (1.0 / 12.0) * living
        masked = states * living
        squares = masked * masked
        add(energy, functools.reduce(lambda a, b: a + b, [squares[:, k * 128 : (k + 1) * 128] for k in range(BLOCK // 128)]), now)
        four = states[:, 0:1]
        for e, at in ((1, 1), (2, BLOCK - 2), (3, BLOCK - 1)):
            four = jnp.where((lane & 3) == e, states[:, at : at + 1], four)
        ends[...] = jnp.where((lane >> 2) == where, four, jnp.zeros_like(four) if now else ends[...])
        stacked(masked, stack)
        rows_hi[...], rows_lo[...] = features(first_pick, second_pick, stack[...], 0, ROWS_PAD)
        right = features(first_pick, second_pick, stack[...], ROWS_PAD, 256)
        for at in range(0, COLS, 256):
            if at + 256 < COLS:
                coming = features(first_pick, second_pick, stack[...], ROWS_PAD + at + 256, 256)
            else:
                cols_hi[:TAIL_QUADS, :], cols_lo[:TAIL_QUADS, :] = features(first_pick, second_pick, stack[...], ROWS_PAD + COLS, TAIL_QUADS)
                side = change[pl.ds(pl.multiple_of(x // 2 * TAIL_SIDES, TAIL_SIDES), TAIL_SIDES), :]
                cols_hi[TAIL_QUADS:, :], cols_lo[TAIL_QUADS:, :] = split2(side)
            value = product(rows_hi[...], rows_lo[...], *right)
            right = coming
            if out is None:
                add(acc, value, now, slice(at, at + 256))
                continue
            value = acc[:, at : at + 256] + value
            for k in range(at // 128, at // 128 + 2):
                out[k * ROWS : (k + 1) * ROWS, :] = value[:ROWS, k * 128 - at : (k + 1) * 128 - at]
        add(tail, product(rows_hi[part, :], rows_lo[part, :], cols_hi[...], cols_lo[...]), now)


def gram_own_kernel(lengths, first_pick, second_pick, mine, theirs, *rest):
    add_blocks(lengths, first_pick, second_pick, (0,), (mine,), (theirs,), rest[:4], rest[4:], True)


def gram_beside_kernel(lengths, first_pick, second_pick, *rest):
    mine, theirs, sums, scratch = rest[:2], rest[2:4], rest[8:12], rest[12:]
    add_blocks(lengths, first_pick, second_pick, (1, 3), mine, theirs, sums, scratch, False)


def gram_across_kernel(lengths, first_pick, second_pick, *rest):
    mine, theirs, given, (out, extra), more, scratch = rest[:1], rest[1:2], rest[2:6], rest[6:8], rest[8:11], rest[11:]
    for ref, value in zip(more, given[1:]):
        ref[...] = value[...]
    sums = (given[0], *more)
    add_blocks(lengths, first_pick, second_pick, (2,), mine, theirs, sums, scratch, False, out)
    _, tail, energy, ends = sums
    out[TAIL_AT : TAIL_AT + TAIL_KEPT, :] = tail[:TAIL_KEPT, :]
    total = lax.dot_general(
        jnp.ones((8, 128), jnp.float32),
        energy[...],
        (NT, ((), ())),
        precision=lax.Precision.HIGHEST,
        preferred_element_type=jnp.float32,
    )
    out[ENERGY_AT:, :] = jnp.concatenate([total, jnp.zeros_like(total)], axis=1)[: TILES - ENERGY_AT, :]
    flat = ends[...].T
    extra[...] = jnp.concatenate([flat[:EXTRA, :], flat[EXTRA : 2 * EXTRA, :]], axis=1)


SUMS = ((ROWS_PAD, COLS), (TAIL_ROWS, 128), (R, 128), (R, 128))
WORK = (
    pltpu.VMEM((4 * R, BLOCK), jnp.bfloat16),
    pltpu.VMEM((R, BLOCK), jnp.float32),
    pltpu.VMEM((ROWS_PAD, BLOCK), jnp.bfloat16),
    pltpu.VMEM((ROWS_PAD, BLOCK), jnp.bfloat16),
    pltpu.VMEM((128, BLOCK), jnp.bfloat16),
    pltpu.VMEM((128, BLOCK), jnp.bfloat16),
)


def gram(lengths, first_pick, second_pick, mine, theirs):
    shapes = tuple(pltpu.VMEM(shape, jnp.float32) for shape in SUMS)
    own = pl.pallas_call(
        gram_own_kernel,
        out_shape=shapes,
        in_specs=[SMEM] + [VMEM] * 4,
        out_specs=(VMEM,) * 4,
        scratch_shapes=WORK,
        compiler_params=ROOM,
        name="gram_own",
    )
    beside = pl.pallas_call(
        gram_beside_kernel,
        out_shape=shapes,
        in_specs=[SMEM] + [VMEM] * 10,
        out_specs=(VMEM,) * 4,
        scratch_shapes=WORK,
        input_output_aliases={7 + k: k for k in range(4)},
        compiler_params=ROOM,
        name="gram_beside",
    )
    across = pl.pallas_call(
        gram_across_kernel,
        out_shape=(pltpu.VMEM((TILES, 128), jnp.float32), pltpu.VMEM((EXTRA, 128), jnp.float32)),
        in_specs=[SMEM] + [VMEM] * 8,
        out_specs=(VMEM, VMEM),
        scratch_shapes=tuple(pltpu.VMEM(shape, jnp.float32) for shape in SUMS[1:]) + WORK,
        compiler_params=ROOM,
        name="gram_across",
    )
    kept = [near_by(v) for v in (first_pick, second_pick)]
    sums = own(lengths, *kept, near_by(mine[0]), near_by(theirs[0]))
    sums = beside(lengths, *kept, *[near_by(v) for v in (mine[1], mine[3], theirs[1], theirs[3], *sums)])
    return across(lengths, *kept, *[near_by(v) for v in (mine[2], theirs[2], *sums)])


def fold_kernel(parts, extra, out):
    out[:PIECE, :] = functools.reduce(lambda a, b: a + b, [parts[k] for k in range(8)])
    out[PIECE:, :] = extra[...]


def fold(parts, extra):
    return pl.pallas_call(
        fold_kernel,
        out_shape=pltpu.VMEM((PIECE + EXTRA, 128), jnp.float32),
        in_specs=[VMEM, VMEM],
        out_specs=VMEM,
        compiler_params=ROOM,
        name="fold",
    )(near_by(parts), near_by(extra))


def weights_of(lengths, energy):
    samples = lengths[0] - 4
    for k in range(1, TRAJ):
        samples += lengths[k] - 4
    samples = samples.astype(jnp.float32)
    inverse = (1.0 / UP) / jnp.sqrt(energy * (1.0 / (UP * UP)) / samples + 1e-06)
    high, middle, low = [part.astype(jnp.float32) for part in split3(inverse)]
    fill = jnp.where(lax.broadcasted_iota(jnp.int32, (8, R), 1) == 0, 1.0, 0.0)
    weights = jnp.concatenate([high, middle, low, fill], axis=1)
    tall = jnp.broadcast_to(weights[0:1, :], (128, 256)).astype(jnp.bfloat16)
    return samples, inverse, weights.astype(jnp.bfloat16), tall


def beyond_ends(lengths, first_pick, second_pick, parts, change):
    x = lax.axis_index("x")
    flat = [parts[k, PIECE:, at : at + R] for k in range(8) for at in (0, R)]
    flat = jnp.concatenate(flat, axis=0)
    ends = jnp.concatenate([flat, flat], axis=1).T[:R, :]
    lane = lax.broadcasted_iota(jnp.int32, (R, 128), 1)
    z, where, e = lane >> 4, (lane >> 2) & 3, lane & 3
    block = where * 8 + z
    before2 = jnp.where(z == 0, pltpu.roll(ends, 18, 1), pltpu.roll(ends, 14, 1))
    before = jnp.where(z == 0, pltpu.roll(ends, 17, 1), pltpu.roll(ends, 13, 1))
    after2 = jnp.where(z == 7, pltpu.roll(ends, 110, 1), pltpu.roll(ends, 114, 1))
    after = jnp.where(z == 7, pltpu.roll(ends, 111, 1), pltpu.roll(ends, 115, 1))
    left = jnp.where(block == 0, 0.0, jnp.where(e == 0, before2 - 8.0 * before, before2))
    right = jnp.where(block == 31, 0.0, jnp.where(e == 3, 8.0 * after - after2, -after2))
    time = block * BLOCK + jnp.where(e < 2, e, BLOCK - 4 + e) + HALF
    owner, offset = (time >> 11) & (TRAJ - 1), time & (SLOT - 1)
    limit = jnp.zeros_like(time)
    for k in range(TRAJ):
        limit = jnp.where(owner == k, lengths[k] - 3, limit)
    living = jnp.where((offset >= 2) & (offset <= limit), 1.0, 0.0)
    change[...] = jnp.where(e < 2, left, right) * (1.0 / 12.0) * living
    high, middle, low = [part.astype(jnp.float32) for part in split3(ends * living)]
    ones = jnp.where(lax.broadcasted_iota(jnp.int32, (R, 128), 0) == 0, 1.0, 0.0)
    stack = jnp.concatenate([high, middle, low, ones], axis=0).astype(jnp.bfloat16)
    part = pl.ds(pl.multiple_of(x % 2 * 128, 128), TAIL_ROWS)
    rows_hi, rows_lo = split2(dot(first_pick[part, :], stack, NN) * dot(second_pick[part, :], stack, NN))
    side = change[pl.ds(pl.multiple_of(x // 2 * TAIL_SIDES, TAIL_SIDES), TAIL_SIDES), :]
    cols_hi, cols_lo = split2(jnp.concatenate([jnp.zeros((TAIL_QUADS, 128), jnp.float32), side], axis=0))
    return product(rows_hi, rows_lo, cols_hi, cols_lo)


def scale_kernel(lengths, first_pick, second_pick, parts, top, bottom, change, row_weight, tail):
    x = lax.axis_index("x")

    def put(at, value):
        cut = min(max(OUT_HALF - at, 0), value.shape[0])
        if cut:
            top[at : at + cut, :] = value[:cut, :]
        if cut < value.shape[0]:
            bottom[at + cut - OUT_HALF : at + value.shape[0] - OUT_HALF, :] = value[cut:, :]

    at = ENERGY_AT - 7 * PIECE
    energy = jnp.broadcast_to(parts[7, at : at + 1, :R], (8, R))
    samples, inverse, weights, tall = weights_of(lengths, energy)
    row_weight[...] = dot(first_pick[:ROWS_PAD, :], tall, NT) * dot(second_pick[:ROWS_PAD, :], tall, NT) / samples
    by_column = (dot(weights, first_pick[ROWS_PAD:, :], NT) * dot(weights, second_pick[ROWS_PAD:, :], NT))[0:1, :]

    def pieces(begin, count):
        at = begin
        while at < begin + count:
            k, row = divmod(at, PIECE)
            size = min(PIECE - row, begin + count - at)
            yield at - begin, size, parts[k, row : row + size, :]
            at += size

    for k in range(COLS // 128):
        for at, size, part in pieces(k * ROWS, ROWS):
            put(k * ROWS_PAD + at, part * row_weight[at : at + size, :] * by_column[:, k * 128 : (k + 1) * 128])
    tail[...] = beyond_ends(lengths, first_pick, second_pick, parts, change)
    for at, size, part in pieces(TAIL_AT, TAIL_KEPT):
        tail[at : at + size, :] = tail[at : at + size, :] + part
    sides = jnp.where(x < 2, inverse[0:1, :TAIL_SIDES], inverse[0:1, TAIL_SIDES:])
    column = jnp.concatenate([by_column[:, COLS:], sides], axis=1)
    tail_rows = jnp.where(x % 2 == 0, row_weight[:TAIL_ROWS, :], row_weight[128:, :])
    put(OUT_TAIL, tail[...] * tail_rows * column)
    for k in range(COLS // 128):
        put(k * ROWS_PAD + ROWS, jnp.zeros((ROWS_PAD - ROWS, 128), jnp.float32))


def scale(lengths, first_pick, second_pick, parts):
    return pl.pallas_call(
        scale_kernel,
        out_shape=(pltpu.VMEM((OUT_HALF, 128), jnp.float32), pltpu.VMEM((OUT_HALF, 128), jnp.float32)),
        in_specs=[SMEM, VMEM, VMEM, VMEM],
        out_specs=(VMEM, VMEM),
        scratch_shapes=[
            pltpu.VMEM((R, 128), jnp.float32),
            pltpu.VMEM((ROWS_PAD, 128), jnp.float32),
            pltpu.VMEM((TAIL_ROWS, 128), jnp.float32),
        ],
        compiler_params=ROOM,
        name="scale",
    )(lengths, *[near_by(v) for v in (first_pick, second_pick, parts)])


def lay_kernel(*refs):
    pieces, (gram_out, side_out, tails, sides) = refs[:8], refs[8:]
    x = lax.axis_index("x")

    def put(source, parts):
        for k in range(COLS // 128):
            first = k * ROWS_PAD
            lanes = pl.ds(pl.multiple_of((source * 4 + k) * 128, 128), 128)
            for part, low, high in parts:
                begin, end = max(first, low), min(first + ROWS, high)
                if begin < end:
                    gram_out[begin - first : end - first, lanes] = part[begin - low : end - low, :]
        for part, low, high in parts:
            begin, end = max(OUT_TAIL, low), min(OUT_ROWS, high)
            if begin < end:
                tails[source, begin - OUT_TAIL : end - OUT_TAIL, :] = part[begin - low : end - low, :]

    for by, top, bottom in zip((0, 3, 1, 2), pieces[::2], pieces[1::2]):
        put((x + by) % 4, [(top, 0, OUT_HALF), (bottom, OUT_HALF, OUT_ROWS)])
    sides[...] = jnp.zeros_like(sides)
    for x_of, low, high in ((0, 0, 128), (1, 128, ROWS)):
        count = high - low
        gram_out[low:high, 16 * 128 :] = tails[x_of, :count, :TAIL_QUADS]
        sides[low:high, :TAIL_SIDES] = tails[x_of, :count, TAIL_QUADS:]
        sides[low:high, TAIL_SIDES:R] = tails[x_of + 2, :count, TAIL_QUADS:]
    side_out[...] = sides[...].T[:R, :ROWS]


def lay(*pieces):
    return pl.pallas_call(
        lay_kernel,
        out_shape=(
            jax.ShapeDtypeStruct((ROWS, FEAT), jnp.float32),
            jax.ShapeDtypeStruct((R, ROWS), jnp.float32),
        ),
        in_specs=[VMEM] * 8,
        out_specs=(VMEM, VMEM),
        scratch_shapes=[pltpu.VMEM((4, TAIL_ROWS, 128), jnp.float32), pltpu.VMEM((384, 128), jnp.float32)],
        compiler_params=ROOM,
        name="lay",
    )(*[near_by(v) for v in pieces])


def ring(top, bottom):
    left_top, right_bottom = turn(top, "x", 1), turn(bottom, "x", 3)
    left_bottom, right_top = turn(bottom, "x", 1), turn(top, "x", 3)
    far_top, far_bottom = turn(left_top, "x", 1), turn(right_bottom, "x", 3)
    return top, bottom, left_top, left_bottom, right_top, right_bottom, far_top, far_bottom


def shards(snapshots, basis, lengths):
    mine, other = project(basis.T, snapshots)
    half = mine + swap(other)
    message = (half + turn(half, "y", 2)) + (turn(half, "y", 1) + turn(half, "y", 3))
    first_pick, second_pick = picks()
    message, first_pick, second_pick = lax.optimization_barrier((message, first_pick, second_pick))
    across = turn(message, "x", 2)
    mine = (message, turn(message, "x", 3), across, turn(message, "x", 1))
    theirs = tuple(swap(part) for part in (mine[0], mine[1], mine[3]))
    theirs = (*theirs[:2], swap(across), theirs[2])
    block, extra = gram(lengths, first_pick, second_pick, mine, theirs)
    piece = fold(lax.all_to_all(block.reshape(8, PIECE, 128), "z", 0, 0, tiled=True), extra)
    parts = everyone(piece, "z").reshape(8, PIECE + EXTRA, 128)
    gram_out, side_out = lay(*ring(*scale(lengths, first_pick, second_pick, parts)))
    return gram_out, side_out.T


def solution(mesh):
    grid = Mesh(mesh.devices.reshape(4, 2, 4, 8), ("y", "c", "x", "z"))
    return jax.shard_map(
        shards,
        mesh=grid,
        in_specs=(P(("y", "c"), ("x", "z")), P(("y", "c"), None), P()),
        out_specs=(P(("y", "c"), None), P(("y", "c"), None)),
        check_vma=False,
    )
```

```python
import functools

import jax
import jax.numpy as jnp
from jax import lax
from jax.experimental import pallas as pl
from jax.experimental.pallas import tpu as pltpu
from jax.sharding import Mesh, PartitionSpec as P


R = 64
FEAT = 2144
SLOT = 2048
TRAJ = 16
BLOCK = 1024
HALF = 512
ROWS = 268
ROWS_PAD = 272
COLS = 512
TAIL_QUADS = 96
TAIL_SIDES = 32
TAIL_ROWS = 144
TAIL_KEPT = 140
PICKS = ROWS_PAD + COLS + TAIL_QUADS
TAIL_AT = 4 * ROWS
PIECE = 152
EXTRA = 8
TILES = 8 * PIECE
ENERGY_AT = TAIL_AT + TAIL_KEPT
OUT_TAIL = 4 * ROWS_PAD
OUT_ROWS = OUT_TAIL + TAIL_ROWS
OUT_HALF = OUT_ROWS // 2
UP = 2.0**16


def swap(value):
    return lax.ppermute(value, "c", [(0, 1), (1, 0)])


def turn(value, axis, by):
    count = lax.axis_size(axis)
    return lax.ppermute(value, axis, [(i, (i + by) % count) for i in range(count)])


def near_by(value):
    return pltpu.with_memory_space_constraint(value, pltpu.VMEM)


def everyone(value, axis):
    count = lax.axis_size(axis)
    spread = jnp.broadcast_to(value[None], (count,) + value.shape)
    return lax.all_to_all(spread, axis, 0, 0, tiled=True)


def one_hots(first_feature, count):
    lane = lax.broadcasted_iota(jnp.int32, (count, 256), 1)
    feature = lax.broadcasted_iota(jnp.int32, (count, 256), 0) + first_feature
    mode = lane & (R - 1)
    below = lane < 3 * R
    ends = R + (mode + 1) * R - (mode + 1) * mode // 2
    passed = jnp.where((lane < R) & (feature >= ends), 1.0, 0.0)
    row = jnp.sum(passed, axis=1, keepdims=True).astype(jnp.int32)
    start = R + row * R - row * (row - 1) // 2
    linear = feature < R
    first = jnp.where(linear, feature, row)
    second = jnp.where(linear, -1, feature - start + row)
    pick_first = below & (mode == first)
    pick_second = (below & (mode == second)) | (linear & (lane == 3 * R))
    as_type = lambda pick: jnp.where(pick, 1.0, 0.0).astype(jnp.bfloat16)
    return as_type(pick_first), as_type(pick_second)


def split3(value):
    high = value.astype(jnp.bfloat16)
    rest = value - high.astype(jnp.float32)
    middle = rest.astype(jnp.bfloat16)
    low = (rest - middle.astype(jnp.float32)).astype(jnp.bfloat16)
    return high, middle, low


def split2(value):
    high = value.astype(jnp.bfloat16)
    return high, (value - high.astype(jnp.float32)).astype(jnp.bfloat16)


def dot(left, right, dims):
    return lax.dot_general(left, right, (dims, ((), ())), preferred_element_type=jnp.float32)


NT = ((1,), (1,))
NN = ((1,), (0,))


def position():
    return lax.axis_index("c"), lax.axis_index("x"), lax.axis_index("z")


def pick_kernel(first_pick, second_pick):
    core, x, _ = position()
    space = lax.axis_index("y") * 2 + core
    for at, count, feature in (
        (0, ROWS_PAD, space * ROWS),
        (ROWS_PAD, COLS, x * COLS),
        (ROWS_PAD + COLS, TAIL_QUADS, 4 * COLS),
    ):
        first, second = one_hots(feature, count)
        first_pick[at : at + count, :] = first
        second_pick[at : at + count, :] = second


SMEM = pl.BlockSpec(memory_space=pltpu.SMEM)
VMEM = pl.BlockSpec(memory_space=pltpu.VMEM)
ROOM = pltpu.CompilerParams(vmem_limit_bytes=24 * 1024 * 1024)


def picks():
    return pl.pallas_call(
        pick_kernel,
        out_shape=(pltpu.VMEM((PICKS, 256), jnp.bfloat16), pltpu.VMEM((PICKS, 256), jnp.bfloat16)),
        out_specs=(VMEM, VMEM),
        compiler_params=ROOM,
        name="picks",
    )()


def whole_block(own, other, core):
    near = jnp.where(core == 0, own[...], other[...])
    far = jnp.where(core == 0, other[...], own[...])
    return jnp.concatenate([near, far], axis=1) * UP


def alive(lengths, start):
    lane = lax.broadcasted_iota(jnp.int32, (1, BLOCK), 1)
    one = lengths[(start + HALF) // SLOT % TRAJ]
    two = lengths[(start + 2 * HALF) // SLOT % TRAJ]
    offset = ((start + HALF) % SLOT + lane) & (SLOT - 1)
    limit = jnp.where(lane < HALF, one, two) - 3
    return jnp.where((offset >= 2) & (offset <= limit), 1.0, 0.0)


def features(first_pick, second_pick, stack, at, count):
    first = dot(first_pick[at : at + count, :], stack, NN)
    second = dot(second_pick[at : at + count, :], stack, NN)
    return split2(first * second)


def product(left_hi, left_lo, right_hi, right_lo):
    return dot(left_hi, right_hi, NT) + dot(left_lo, right_hi, NT) + dot(left_hi, right_lo, NT)


def stacked(masked, stack):
    stack[:R, :], stack[R : 2 * R, :], stack[2 * R : 3 * R, :] = split3(masked)
    index = lax.broadcasted_iota(jnp.int32, masked.shape, 0)
    stack[3 * R :, :] = jnp.where(index == 0, 1.0, 0.0).astype(jnp.bfloat16)


def project_kernel(basis, snapshots, mine, other, basis_in, cells, total, arrived):
    core = lax.axis_index("c")
    parts = cells.shape[0]
    size = BLOCK // parts
    first = pltpu.make_async_copy(basis, basis_in, arrived.at[parts])
    loads = [
        pltpu.make_async_copy(snapshots.at[pl.ds(k * size, size), :], cells.at[k], arrived.at[k]) for k in range(parts)
    ]
    first.start()
    for load in loads:
        load.start()
    first.wait()
    for k, load in enumerate(loads):
        load.wait()
        part = dot(basis_in[:, k * size : (k + 1) * size], cells[k], NN)
        total[...] = part if k == 0 else total[...] + part
    low, high = total[:, :HALF], total[:, HALF:]
    mine[...] = jnp.where(core == 0, low, high)
    other[...] = jnp.where(core == 0, high, low)


def project(basis, snapshots):
    parts = 4
    return pl.pallas_call(
        project_kernel,
        out_shape=(pltpu.VMEM((R, HALF), jnp.float32), pltpu.VMEM((R, HALF), jnp.float32)),
        in_specs=[pl.BlockSpec(memory_space=pltpu.HBM)] * 2,
        out_specs=(VMEM, VMEM),
        scratch_shapes=[
            pltpu.VMEM((R, BLOCK), jnp.bfloat16),
            pltpu.VMEM((parts, BLOCK // parts, BLOCK), jnp.bfloat16),
            pltpu.VMEM((R, BLOCK), jnp.float32),
            pltpu.SemaphoreType.DMA((parts + 1,)),
        ],
        compiler_params=ROOM,
        name="project",
    )(*[pltpu.with_memory_space_constraint(v, pltpu.HBM) for v in (basis, snapshots)])


def stacked(masked, stack):
    stack[:R, :], stack[R : 2 * R, :], stack[2 * R : 3 * R, :] = split3(masked)
    index = lax.broadcasted_iota(jnp.int32, masked.shape, 0)
    stack[3 * R :, :] = jnp.where(index == 0, 1.0, 0.0).astype(jnp.bfloat16)


def add_blocks(lengths, first_pick, second_pick, steps, mine, theirs, sums, scratch, fresh, out=None):
    acc, tail, energy, ends = sums
    stack, change, rows_hi, rows_lo, cols_hi, cols_lo = scratch
    core, x, z = position()
    wide = lax.broadcasted_iota(jnp.int32, (R, BLOCK), 1)
    lane = lax.broadcasted_iota(jnp.int32, (R, 128), 1)
    part = pl.ds(pl.multiple_of(x % 2 * 128, 128), TAIL_ROWS)

    def add(ref, value, now, at=slice(None)):
        ref[:, at] = value if now else ref[:, at] + value

    for index, step in enumerate(steps):
        now = fresh and index == 0
        where = (x + step) % 4
        states = whole_block(mine[index], theirs[index], core)
        living = alive(lengths, (where * 8 + z) * BLOCK)
        before = jnp.where(wide < 1, 0.0, pltpu.roll(states, 1, 1))
        before2 = jnp.where(wide < 2, 0.0, pltpu.roll(states, 2, 1))
        after = jnp.where(wide >= BLOCK - 1, 0.0, pltpu.roll(states, BLOCK - 1, 1))
        after2 = jnp.where(wide >= BLOCK - 2, 0.0, pltpu.roll(states, BLOCK - 2, 1))
        change[...] = (before2 - 8.0 * before + 8.0 * after - after2) * (1.0 / 12.0) * living
        masked = states * living
        squares = masked * masked
        add(energy, functools.reduce(lambda a, b: a + b, [squares[:, k * 128 : (k + 1) * 128] for k in range(BLOCK // 128)]), now)
        four = states[:, 0:1]
        for e, at in ((1, 1), (2, BLOCK - 2), (3, BLOCK - 1)):
            four = jnp.where((lane & 3) == e, states[:, at : at + 1], four)
        ends[...] = jnp.where((lane >> 2) == where, four, jnp.zeros_like(four) if now else ends[...])
        stacked(masked, stack)
        rows_hi[...], rows_lo[...] = features(first_pick, second_pick, stack[...], 0, ROWS_PAD)
        right = features(first_pick, second_pick, stack[...], ROWS_PAD, 256)
        for at in range(0, COLS, 256):
            if at + 256 < COLS:
                coming = features(first_pick, second_pick, stack[...], ROWS_PAD + at + 256, 256)
            else:
                cols_hi[:TAIL_QUADS, :], cols_lo[:TAIL_QUADS, :] = features(first_pick, second_pick, stack[...], ROWS_PAD + COLS, TAIL_QUADS)
                side = change[pl.ds(pl.multiple_of(x // 2 * TAIL_SIDES, TAIL_SIDES), TAIL_SIDES), :]
                cols_hi[TAIL_QUADS:, :], cols_lo[TAIL_QUADS:, :] = split2(side)
            value = product(rows_hi[...], rows_lo[...], *right)
            right = coming
            if out is None:
                add(acc, value, now, slice(at, at + 256))
                continue
            value = acc[:, at : at + 256] + value
            for k in range(at // 128, at // 128 + 2):
                out[k * ROWS : (k + 1) * ROWS, :] = value[:ROWS, k * 128 - at : (k + 1) * 128 - at]
        add(tail, product(rows_hi[part, :], rows_lo[part, :], cols_hi[...], cols_lo[...]), now)


def gram_own_kernel(lengths, first_pick, second_pick, mine, theirs, *rest):
    add_blocks(lengths, first_pick, second_pick, (0,), (mine,), (theirs,), rest[:4], rest[4:], True)


def gram_beside_kernel(lengths, first_pick, second_pick, *rest):
    mine, theirs, sums, scratch = rest[:2], rest[2:4], rest[8:12], rest[12:]
    add_blocks(lengths, first_pick, second_pick, (1, 3), mine, theirs, sums, scratch, False)


def gram_across_kernel(lengths, first_pick, second_pick, *rest):
    mine, theirs, given, (out, extra), more, scratch = rest[:1], rest[1:2], rest[2:6], rest[6:8], rest[8:11], rest[11:]
    for ref, value in zip(more, given[1:]):
        ref[...] = value[...]
    sums = (given[0], *more)
    add_blocks(lengths, first_pick, second_pick, (2,), mine, theirs, sums, scratch, False, out)
    _, tail, energy, ends = sums
    out[TAIL_AT : TAIL_AT + TAIL_KEPT, :] = tail[:TAIL_KEPT, :]
    total = lax.dot_general(
        jnp.ones((8, 128), jnp.float32),
        energy[...],
        (NT, ((), ())),
        precision=lax.Precision.HIGHEST,
        preferred_element_type=jnp.float32,
    )
    out[ENERGY_AT:, :] = jnp.concatenate([total, jnp.zeros_like(total)], axis=1)[: TILES - ENERGY_AT, :]
    flat = ends[...].T
    extra[...] = jnp.concatenate([flat[:EXTRA, :], flat[EXTRA : 2 * EXTRA, :]], axis=1)


SUMS = ((ROWS_PAD, COLS), (TAIL_ROWS, 128), (R, 128), (R, 128))
WORK = (
    pltpu.VMEM((4 * R, BLOCK), jnp.bfloat16),
    pltpu.VMEM((R, BLOCK), jnp.float32),
    pltpu.VMEM((ROWS_PAD, BLOCK), jnp.bfloat16),
    pltpu.VMEM((ROWS_PAD, BLOCK), jnp.bfloat16),
    pltpu.VMEM((128, BLOCK), jnp.bfloat16),
    pltpu.VMEM((128, BLOCK), jnp.bfloat16),
)


def gram(lengths, first_pick, second_pick, mine, theirs):
    shapes = tuple(pltpu.VMEM(shape, jnp.float32) for shape in SUMS)
    own = pl.pallas_call(
        gram_own_kernel,
        out_shape=shapes,
        in_specs=[SMEM] + [VMEM] * 4,
        out_specs=(VMEM,) * 4,
        scratch_shapes=WORK,
        compiler_params=ROOM,
        name="gram_own",
    )
    beside = pl.pallas_call(
        gram_beside_kernel,
        out_shape=shapes,
        in_specs=[SMEM] + [VMEM] * 10,
        out_specs=(VMEM,) * 4,
        scratch_shapes=WORK,
        input_output_aliases={7 + k: k for k in range(4)},
        compiler_params=ROOM,
        name="gram_beside",
    )
    across = pl.pallas_call(
        gram_across_kernel,
        out_shape=(pltpu.VMEM((TILES, 128), jnp.float32), pltpu.VMEM((EXTRA, 128), jnp.float32)),
        in_specs=[SMEM] + [VMEM] * 8,
        out_specs=(VMEM, VMEM),
        scratch_shapes=tuple(pltpu.VMEM(shape, jnp.float32) for shape in SUMS[1:]) + WORK,
        compiler_params=ROOM,
        name="gram_across",
    )
    kept = [near_by(v) for v in (first_pick, second_pick)]
    sums = own(lengths, *kept, near_by(mine[0]), near_by(theirs[0]))
    sums = beside(lengths, *kept, *[near_by(v) for v in (mine[1], mine[3], theirs[1], theirs[3], *sums)])
    return across(lengths, *kept, *[near_by(v) for v in (mine[2], theirs[2], *sums)])


def fold_kernel(parts, extra, out):
    out[:PIECE, :] = functools.reduce(lambda a, b: a + b, [parts[k] for k in range(8)])
    out[PIECE:, :] = extra[...]


def fold(parts, extra):
    return pl.pallas_call(
        fold_kernel,
        out_shape=pltpu.VMEM((PIECE + EXTRA, 128), jnp.float32),
        in_specs=[VMEM, VMEM],
        out_specs=VMEM,
        compiler_params=ROOM,
        name="fold",
    )(near_by(parts), near_by(extra))


def weights_of(lengths, energy):
    samples = lengths[0] - 4
    for k in range(1, TRAJ):
        samples += lengths[k] - 4
    samples = samples.astype(jnp.float32)
    inverse = (1.0 / UP) / jnp.sqrt(energy * (1.0 / (UP * UP)) / samples + 1e-06)
    high, middle, low = [part.astype(jnp.float32) for part in split3(inverse)]
    fill = jnp.where(lax.broadcasted_iota(jnp.int32, (8, R), 1) == 0, 1.0, 0.0)
    weights = jnp.concatenate([high, middle, low, fill], axis=1)
    tall = jnp.broadcast_to(weights[0:1, :], (128, 256)).astype(jnp.bfloat16)
    return samples, inverse, weights.astype(jnp.bfloat16), tall


def beyond_ends(lengths, first_pick, second_pick, parts, change):
    x = lax.axis_index("x")
    flat = [parts[k, PIECE:, at : at + R] for k in range(8) for at in (0, R)]
    flat = jnp.concatenate(flat, axis=0)
    ends = jnp.concatenate([flat, flat], axis=1).T[:R, :]
    lane = lax.broadcasted_iota(jnp.int32, (R, 128), 1)
    z, where, e = lane >> 4, (lane >> 2) & 3, lane & 3
    block = where * 8 + z
    before2 = jnp.where(z == 0, pltpu.roll(ends, 18, 1), pltpu.roll(ends, 14, 1))
    before = jnp.where(z == 0, pltpu.roll(ends, 17, 1), pltpu.roll(ends, 13, 1))
    after2 = jnp.where(z == 7, pltpu.roll(ends, 110, 1), pltpu.roll(ends, 114, 1))
    after = jnp.where(z == 7, pltpu.roll(ends, 111, 1), pltpu.roll(ends, 115, 1))
    left = jnp.where(block == 0, 0.0, jnp.where(e == 0, before2 - 8.0 * before, before2))
    right = jnp.where(block == 31, 0.0, jnp.where(e == 3, 8.0 * after - after2, -after2))
    time = block * BLOCK + jnp.where(e < 2, e, BLOCK - 4 + e) + HALF
    owner, offset = (time >> 11) & (TRAJ - 1), time & (SLOT - 1)
    limit = jnp.zeros_like(time)
    for k in range(TRAJ):
        limit = jnp.where(owner == k, lengths[k] - 3, limit)
    living = jnp.where((offset >= 2) & (offset <= limit), 1.0, 0.0)
    change[...] = jnp.where(e < 2, left, right) * (1.0 / 12.0) * living
    high, middle, low = [part.astype(jnp.float32) for part in split3(ends * living)]
    ones = jnp.where(lax.broadcasted_iota(jnp.int32, (R, 128), 0) == 0, 1.0, 0.0)
    stack = jnp.concatenate([high, middle, low, ones], axis=0).astype(jnp.bfloat16)
    part = pl.ds(pl.multiple_of(x % 2 * 128, 128), TAIL_ROWS)
    rows_hi, rows_lo = split2(dot(first_pick[part, :], stack, NN) * dot(second_pick[part, :], stack, NN))
    side = change[pl.ds(pl.multiple_of(x // 2 * TAIL_SIDES, TAIL_SIDES), TAIL_SIDES), :]
    cols_hi, cols_lo = split2(jnp.concatenate([jnp.zeros((TAIL_QUADS, 128), jnp.float32), side], axis=0))
    return product(rows_hi, rows_lo, cols_hi, cols_lo)


def scale_kernel(lengths, first_pick, second_pick, parts, top, bottom, change, row_weight, tail):
    x = lax.axis_index("x")

    def put(at, value):
        cut = min(max(OUT_HALF - at, 0), value.shape[0])
        if cut:
            top[at : at + cut, :] = value[:cut, :]
        if cut < value.shape[0]:
            bottom[at + cut - OUT_HALF : at + value.shape[0] - OUT_HALF, :] = value[cut:, :]

    at = ENERGY_AT - 7 * PIECE
    energy = jnp.broadcast_to(parts[7, at : at + 1, :R], (8, R))
    samples, inverse, weights, tall = weights_of(lengths, energy)
    row_weight[...] = dot(first_pick[:ROWS_PAD, :], tall, NT) * dot(second_pick[:ROWS_PAD, :], tall, NT) / samples
    by_column = (dot(weights, first_pick[ROWS_PAD:, :], NT) * dot(weights, second_pick[ROWS_PAD:, :], NT))[0:1, :]

    def pieces(begin, count):
        at = begin
        while at < begin + count:
            k, row = divmod(at, PIECE)
            size = min(PIECE - row, begin + count - at)
            yield at - begin, size, parts[k, row : row + size, :]
            at += size

    for k in range(COLS // 128):
        for at, size, part in pieces(k * ROWS, ROWS):
            put(k * ROWS_PAD + at, part * row_weight[at : at + size, :] * by_column[:, k * 128 : (k + 1) * 128])
    tail[...] = beyond_ends(lengths, first_pick, second_pick, parts, change)
    for at, size, part in pieces(TAIL_AT, TAIL_KEPT):
        tail[at : at + size, :] = tail[at : at + size, :] + part
    sides = jnp.where(x < 2, inverse[0:1, :TAIL_SIDES], inverse[0:1, TAIL_SIDES:])
    column = jnp.concatenate([by_column[:, COLS:], sides], axis=1)
    tail_rows = jnp.where(x % 2 == 0, row_weight[:TAIL_ROWS, :], row_weight[128:, :])
    put(OUT_TAIL, tail[...] * tail_rows * column)
    for k in range(COLS // 128):
        put(k * ROWS_PAD + ROWS, jnp.zeros((ROWS_PAD - ROWS, 128), jnp.float32))


def scale(lengths, first_pick, second_pick, parts):
    return pl.pallas_call(
        scale_kernel,
        out_shape=(pltpu.VMEM((OUT_HALF, 128), jnp.float32), pltpu.VMEM((OUT_HALF, 128), jnp.float32)),
        in_specs=[SMEM, VMEM, VMEM, VMEM],
        out_specs=(VMEM, VMEM),
        scratch_shapes=[
            pltpu.VMEM((R, 128), jnp.float32),
            pltpu.VMEM((ROWS_PAD, 128), jnp.float32),
            pltpu.VMEM((TAIL_ROWS, 128), jnp.float32),
        ],
        compiler_params=ROOM,
        name="scale",
    )(lengths, *[near_by(v) for v in (first_pick, second_pick, parts)])


def lay_kernel(*refs):
    pieces, (gram_out, side_out, staged, edge, side, tails, sides, done) = refs[:8], refs[8:]
    x = lax.axis_index("x")
    copies = []

    def send(value, target):
        copies.append(pltpu.make_async_copy(value, target, done.at[len(copies)]))
        copies[-1].start()

    for index, by in enumerate((0, 3, 1, 2)):
        source = (x + by) % 4
        parts = [(pieces[2 * index], 0, OUT_HALF), (pieces[2 * index + 1], OUT_HALF, OUT_ROWS)]
        for k in range(COLS // 128):
            first = k * ROWS_PAD
            for part, low, high in parts:
                begin, end = max(first, low), min(first + ROWS, high)
                if begin < end:
                    staged[index, begin - first : end - first, k * 128 : (k + 1) * 128] = part[begin - low : end - low, :]
        send(staged.at[index], gram_out.at[:, pl.ds(pl.multiple_of(source * COLS, COLS), COLS)])
        for part, low, high in parts:
            begin, end = max(OUT_TAIL, low), min(OUT_ROWS, high)
            if begin < end:
                tails[source, begin - OUT_TAIL : end - OUT_TAIL, :] = part[begin - low : end - low, :]
    sides[...] = jnp.zeros_like(sides)
    for x_of, low, high in ((0, 0, 128), (1, 128, ROWS)):
        count = high - low
        edge[low:high, :] = tails[x_of, :count, :TAIL_QUADS]
        sides[low:high, :TAIL_SIDES] = tails[x_of, :count, TAIL_QUADS:]
        sides[low:high, TAIL_SIDES:R] = tails[x_of + 2, :count, TAIL_QUADS:]
    send(edge, gram_out.at[:, pl.ds(4 * COLS, TAIL_QUADS)])
    side[...] = sides[...].T[:R, :ROWS]
    send(side, side_out)
    for copy in copies:
        copy.wait()


def lay(*pieces):
    whole = pl.BlockSpec(memory_space=pltpu.HBM)
    return pl.pallas_call(
        lay_kernel,
        out_shape=(pltpu.HBM((ROWS, FEAT), jnp.float32), pltpu.HBM((R, ROWS), jnp.float32)),
        in_specs=[VMEM] * 8,
        out_specs=(whole, whole),
        scratch_shapes=[
            pltpu.VMEM((4, ROWS, COLS), jnp.float32),
            pltpu.VMEM((ROWS, TAIL_QUADS), jnp.float32),
            pltpu.VMEM((R, ROWS), jnp.float32),
            pltpu.VMEM((4, TAIL_ROWS, 128), jnp.float32),
            pltpu.VMEM((384, 128), jnp.float32),
            pltpu.SemaphoreType.DMA((6,)),
        ],
        compiler_params=ROOM,
        name="lay",
    )(*[near_by(v) for v in pieces])


def ring(top, bottom):
    left_top, right_bottom = turn(top, "x", 1), turn(bottom, "x", 3)
    left_bottom, right_top = turn(bottom, "x", 1), turn(top, "x", 3)
    far_top, far_bottom = turn(left_top, "x", 1), turn(right_bottom, "x", 3)
    return top, bottom, left_top, left_bottom, right_top, right_bottom, far_top, far_bottom


def shards(snapshots, basis, lengths):
    mine, other = project(basis.T, snapshots)
    half = mine + swap(other)
    message = (half + turn(half, "y", 2)) + (turn(half, "y", 1) + turn(half, "y", 3))
    first_pick, second_pick = picks()
    message, first_pick, second_pick = lax.optimization_barrier((message, first_pick, second_pick))
    across = turn(message, "x", 2)
    mine = (message, turn(message, "x", 3), across, turn(message, "x", 1))
    theirs = tuple(swap(part) for part in (mine[0], mine[1], mine[3]))
    theirs = (*theirs[:2], swap(across), theirs[2])
    block, extra = gram(lengths, first_pick, second_pick, mine, theirs)
    piece = fold(lax.all_to_all(block.reshape(8, PIECE, 128), "z", 0, 0, tiled=True), extra)
    parts = everyone(piece, "z").reshape(8, PIECE + EXTRA, 128)
    gram_out, side_out = lay(*ring(*scale(lengths, first_pick, second_pick, parts)))
    return gram_out, side_out.T


def solution(mesh):
    grid = Mesh(mesh.devices.reshape(4, 2, 4, 8), ("y", "c", "x", "z"))
    return jax.shard_map(
        shards,
        mesh=grid,
        in_specs=(P(("y", "c"), ("x", "z")), P(("y", "c"), None), P()),
        out_specs=(P(("y", "c"), None), P(("y", "c"), None)),
        check_vma=False,
    )
```
